32 devices in a mesh: groups: 2 (over y), lon: 4 (over z), lat: 2 (over x), segment: 2 (over core).
Axes of the slice: x: 2, y: 2, z: 4, core: 2. Of those that a mesh axis runs over, the one named last changes fastest.
Arguments:
- inputs: bfloat16 [32, 128, 512], P(('groups', 'lat'), 'lon'), parts along dimension 0, may hold values from -6 to 6
- cotangent: bfloat16 [32, 128, 512], P(('groups', 'lat'), 'lon'), parts along dimension 0, may hold values from -8 to 8
- kernel: bfloat16 [2, 49, 512], P('segment'), may hold values from -0.875 to 0.875
- conv_bias: float32 [2, 512], P('segment'), may hold values from -3 to 3
- norm_gain: float32 [2, 512], P('segment'), may hold values from 0.5 to 2
- norm_shift: float32 [2, 512], P('segment'), may hold values from -3 to 3
- up_weight: bfloat16 [2, 512, 2048], P('segment'), may hold values from -0.25 to 0.25
- hidden_bias: float32 [2, 2048], P('segment'), may hold values from -3 to 3
- down_weight: bfloat16 [2, 2048, 512], P('segment'), may hold values from -0.125 to 0.125
- out_bias: float32 [2, 512], P('segment'), may hold values from -3 to 3
- layer_scale: float32 [2, 512], P('segment'), may hold values from 0.5 to 1.5
Outputs:
- section_out: bfloat16 [2, 32, 128, 512], P('segment', ('groups', 'lat'), 'lon'), parts along dimension 1
- boundary_grad: bfloat16 [2, 32, 128, 512], P('segment', ('groups', 'lat'), 'lon'), parts along dimension 1
- up_grad: float32 [4, 512, 2048], P(('groups', 'segment'), None, ('lon', 'lat')), parts along dimension 0
- down_grad: float32 [4, 2048, 512], P(('groups', 'segment'), ('lon', 'lat')), parts along dimension 0
- hidden_bias_grad: float32 [4, 2048], P(('groups', 'segment'), ('lon', 'lat')), parts along dimension 0
- kernel_grad: float32 [4, 49, 512], P(('groups', 'segment'), None, ('lon', 'lat')), parts along dimension 0
- vector_grad: float32 [4, 5, 512], P(('groups', 'segment'), None, ('lon', 'lat')), parts along dimension 0
The draws below stay inside these ranges and needn't reach their ends.
There are 2 independent parts, one for each index of `groups`. The reference program is written for one: setup_inputs(seed, part) draws one part's arguments, and reference() takes and returns one part's arrays. A program takes and returns all parts, laid end to end along the dimension named above; an argument that names none is the same for every part. Nothing has to cross between parts.
All inputs are finite; a program needn't handle non-finite values.
Results may differ from the reference program's by a relative error of at most 0.023.
Values may be sent and summed in bfloat16 or wider, within the bound.
A program may use at most 128 MiB of HBM per device.

```python
import math
import jax
import jax.numpy as jnp
from jax import lax

C = 512
HID = 2048
KERNEL = 7
SECTIONS = 2
LAT = 16
LON = 128


def spiked(values, own_key, source, target, shards_of, factor):
    def block_of(axis_at):
        return (jnp.arange(values.shape[axis_at]) // (values.shape[axis_at] // shards_of)).reshape((-1,) + (1,) * (values.ndim - 1 - axis_at))

    near = jax.random.permutation(own_key, shards_of)[block_of(target)]
    other_side = (block_of(target) + shards_of // 2) % shards_of
    return jnp.where((block_of(source) == near) | (block_of(source) == other_side), factor * values, values)


def block_scale(own_key, shape, pieces, smallest, high):
    level, own = 1.0, jax.random.fold_in(own_key, 6)
    for axis_at, shards_of in pieces:
        heights = jnp.exp(jax.random.uniform(jax.random.fold_in(own, axis_at), (shards_of,), jnp.float32, smallest / len(pieces), high / len(pieces)))
        level = level * jnp.repeat(heights, shape[axis_at] // shards_of).reshape([-1 if axis == axis_at else 1 for axis in range(len(shape))])
    return level


def scatter_about(stream_key, extent, width, limit, split=(), dtype=jnp.bfloat16):
    gain = block_scale(stream_key, extent, split, -0.22, 0.18) if split else 1.0
    array = jax.random.normal(stream_key, extent, jnp.float32) * width * gain
    return jnp.minimum(jnp.maximum(array, -limit), limit).astype(dtype)


def noise_with(rng, extent, deviation, reach, cuts, heavy, held_as=jnp.bfloat16):
    values = deviation * jax.random.normal(rng, extent, jnp.float32)
    if cuts:
        values = values * block_scale(rng, extent, cuts, -0.22, 0.18)
    return jnp.clip(spiked(values, jax.random.fold_in(rng, 3), *heavy), -reach, reach).astype(held_as)


def setup_inputs(seed: int = 0, part: int = 0) -> dict:
    key_list = jax.random.split(jax.random.key(seed), 12)
    part_keys = jax.random.split(jax.random.fold_in(key_list[11], part), 12)
    inputs = scatter_about(part_keys[0], (LAT, LON, C), 1.0, 6.0, ((0, 2), (1, 4)))
    cotangent = noise_with(part_keys[1], (LAT, LON, C), 1.0, 8.0, ((0, 2), (1, 4)), (1, 2, 4, 2.0))
    kernel = scatter_about(key_list[2], (SECTIONS, KERNEL * KERNEL, C), (KERNEL * KERNEL) ** -0.5, 0.875, ((0, 2),))
    conv_bias = scatter_about(key_list[3], (SECTIONS, C), 0.5, 3.0, ((0, 2),), jnp.float32)
    norm_gain = jnp.clip(jnp.exp(math.log(2.0) - 1.3862944 * jax.random.uniform(key_list[4], (SECTIONS, C), jnp.float32) ** block_scale(key_list[4], (SECTIONS, C), ((0, 2),), -0.2, 0.2)), 0.5, 2.0)
    norm_shift = scatter_about(key_list[5], (SECTIONS, C), 0.5, 3.0, ((0, 2),), jnp.float32)
    up_weight = scatter_about(key_list[6], (SECTIONS, C, HID), C ** -0.5, 0.25, ((0, 2),))
    hidden_bias = scatter_about(key_list[7], (SECTIONS, HID), 0.5, 3.0, ((0, 2),), jnp.float32)
    down_weight = scatter_about(key_list[8], (SECTIONS, HID, C), HID ** -0.5, 0.125, ((0, 2),))
    out_bias = scatter_about(key_list[9], (SECTIONS, C), 0.5, 3.0, ((0, 2),), jnp.float32)
    layer_scale = jnp.clip(0.5 + 1.0 * jax.random.uniform(key_list[10], (SECTIONS, C), jnp.float32) ** block_scale(key_list[10], (SECTIONS, C), ((0, 2),), -0.2, 0.2), 0.5, 1.5)
    return dict(inputs=inputs, cotangent=cotangent, kernel=kernel, conv_bias=conv_bias, norm_gain=norm_gain, norm_shift=norm_shift, up_weight=up_weight, hidden_bias=hidden_bias, down_weight=down_weight, out_bias=out_bias, layer_scale=layer_scale)


EPSILON = 1e-06
ROOT_HALF = 0.7071067811865476
DENSITY_SCALE = 0.3989422804014327

def extend_field(values):
    margin = KERNEL // 2
    half_turn = values.shape[1] // 2
    northern = jnp.roll(values[:margin][::-1], half_turn, axis=1)
    southern = jnp.roll(values[-margin:][::-1], half_turn, axis=1)
    lat_extended = jnp.concatenate([northern, values, southern], axis=0)
    return jnp.concatenate([lat_extended[:, -margin:], lat_extended, lat_extended[:, :margin]], axis=1)

def correlate(padded, stencil, out_rows, out_cols):
    accumulated = jnp.zeros((out_rows, out_cols, padded.shape[2]), jnp.float32)
    for row_tap in range(KERNEL):
        for col_tap in range(KERNEL):
            window = padded[row_tap:row_tap + out_rows, col_tap:col_tap + out_cols].astype(jnp.float32)
            accumulated = accumulated + window * stencil[row_tap, col_tap].astype(jnp.float32)
    return accumulated

def stencil_terms(padded, grad_low, out_rows, out_cols):
    grad_wide = grad_low.astype(jnp.float32)
    columns = []
    for row_tap in range(KERNEL):
        for col_tap in range(KERNEL):
            window = padded[row_tap:row_tap + out_rows, col_tap:col_tap + out_cols].astype(jnp.float32)
            columns.append(lax.optimization_barrier(jnp.sum(window * grad_wide, axis=(0, 1))))
    return jnp.stack(columns)

def gelu_parts(before):
    cumulative = 0.5 * (1.0 + lax.erf(before * ROOT_HALF))
    density = jnp.exp(-0.5 * before * before) * DENSITY_SCALE
    return (before * cumulative, cumulative + before * density)

def forward_section(values, padded, params):
    stencil, conv_bias, norm_gain, norm_shift, up_matrix, bias_hidden, down_matrix, bias_out, scaling = params
    out_rows, out_cols, channels = values.shape
    stencil_grid = stencil.reshape(KERNEL, KERNEL, channels)
    activity = correlate(padded, stencil_grid, out_rows, out_cols) + conv_bias
    average = lax.optimization_barrier(jnp.mean(activity, axis=-1, keepdims=True))
    centred = activity - average
    variance = lax.optimization_barrier(jnp.mean(centred * centred, axis=-1, keepdims=True))
    inverse = lax.rsqrt(variance + EPSILON)
    unit_norm = centred * inverse
    normed = (unit_norm * norm_gain + norm_shift).astype(jnp.bfloat16).reshape(out_rows * out_cols, channels)
    before = jnp.dot(normed, up_matrix, preferred_element_type=jnp.float32) + bias_hidden
    activated, slope_value = gelu_parts(before)
    hidden = activated.astype(jnp.bfloat16)
    branch = jnp.dot(hidden, down_matrix, preferred_element_type=jnp.float32) + bias_out
    result = (values.astype(jnp.float32) + scaling * branch.reshape(out_rows, out_cols, channels)).astype(jnp.bfloat16)
    return (result, (padded, unit_norm, inverse, normed, slope_value, hidden, branch))

def backward_section(stored, upstream, params, extender, north_weight, south_weight):
    padded, unit_norm, inverse, normed, slope_value, hidden, branch = stored
    stencil, conv_bias, norm_gain, norm_shift, up_matrix, bias_hidden, down_matrix, bias_out, scaling = params
    out_rows, out_cols, channels = upstream.shape
    margin = KERNEL // 2
    incoming = upstream.astype(jnp.float32)
    incoming_flat = incoming.reshape(out_rows * out_cols, channels)
    scale_grad = lax.optimization_barrier(jnp.sum(incoming_flat * branch, axis=0))
    scaled = (incoming_flat * scaling).astype(jnp.bfloat16)
    bias_out_grad = lax.optimization_barrier(jnp.sum(scaled.astype(jnp.float32), axis=0))
    down_sum = jnp.dot(hidden.T, scaled, preferred_element_type=jnp.float32)
    hidden_grad = jnp.dot(scaled, down_matrix.T, preferred_element_type=jnp.float32)
    before_grad = (hidden_grad * slope_value).astype(jnp.bfloat16)
    up_sum = jnp.dot(normed.T, before_grad, preferred_element_type=jnp.float32)
    bias_sum = lax.optimization_barrier(jnp.sum(before_grad.astype(jnp.float32), axis=0))
    normed_grad = jnp.dot(before_grad, up_matrix.T, preferred_element_type=jnp.float32).reshape(out_rows, out_cols, channels)
    gain_grad = lax.optimization_barrier(jnp.sum(normed_grad * unit_norm, axis=(0, 1)))
    shift_grad = lax.optimization_barrier(jnp.sum(normed_grad, axis=(0, 1)))
    gained = normed_grad * norm_gain
    activity_grad = inverse * (gained - lax.optimization_barrier(jnp.mean(gained, axis=-1, keepdims=True)) - unit_norm * lax.optimization_barrier(jnp.mean(gained * unit_norm, axis=-1, keepdims=True)))
    activity_low = activity_grad.astype(jnp.bfloat16)
    conv_bias_grad = lax.optimization_barrier(jnp.sum(activity_low.astype(jnp.float32), axis=(0, 1)))
    stencil_sum = stencil_terms(padded, activity_low, out_rows, out_cols)
    spread = extender(activity_low)
    stencil_grid = stencil.reshape(KERNEL, KERNEL, channels).astype(jnp.float32)
    flipped = stencil_grid[::-1, ::-1]
    correction = stencil_grid[:, ::-1] - flipped
    through = correlate(spread, flipped, out_rows, out_cols)
    zero_rows = jnp.zeros_like(spread[:2 * margin])
    top_part = jnp.concatenate([spread[:margin], zero_rows], axis=0)
    bottom_part = jnp.concatenate([zero_rows, spread[-margin:]], axis=0)
    top_fix = correlate(top_part, correction, margin, out_cols) * north_weight
    bottom_fix = correlate(bottom_part, correction, margin, out_cols) * south_weight
    rest_rows = out_rows - margin
    top_full = jnp.pad(top_fix, ((0, rest_rows), (0, 0), (0, 0)))
    bottom_full = jnp.pad(bottom_fix, ((rest_rows, 0), (0, 0), (0, 0)))
    through = through + top_full + bottom_full
    passed = (incoming + through).astype(jnp.bfloat16)
    vectors = jnp.stack([conv_bias_grad, gain_grad, shift_grad, bias_out_grad, scale_grad])
    return (passed, (up_sum, down_sum, bias_sum, stencil_sum, vectors))

def reference(inputs, cotangent, kernel, conv_bias, norm_gain, norm_shift, up_weight, hidden_bias, down_weight, out_bias, layer_scale):

    def section_params(index):
        return (kernel[index], conv_bias[index], norm_gain[index], norm_shift[index], up_weight[index], hidden_bias[index], down_weight[index], out_bias[index], layer_scale[index])
    first_out, first_stored = forward_section(inputs, extend_field(inputs), section_params(0))
    second_out, second_stored = forward_section(first_out, extend_field(first_out), section_params(1))
    second_grad, second_sums = backward_section(second_stored, cotangent, section_params(1), extend_field, 1.0, 1.0)
    first_grad, first_sums = backward_section(first_stored, second_grad, section_params(0), extend_field, 1.0, 1.0)
    return (jnp.stack([first_out, second_out]), jnp.stack([first_grad, second_grad]), jnp.stack([first_sums[0], second_sums[0]]), jnp.stack([first_sums[1], second_sums[1]]), jnp.stack([first_sums[2], second_sums[2]]), jnp.stack([first_sums[3], second_sums[3]]), jnp.stack([first_sums[4], second_sums[4]]))
```

```python
import functools
import types
import jax
import jax.numpy as jnp
from jax import lax
from jax.experimental import pallas as pl
from jax.experimental.pallas import tpu as pltpu
from jax.sharding import PartitionSpec as P

KERNEL = 7
MARGIN = KERNEL // 2
EPSILON = 1e-06
ROOT_HALF = 0.7071067811865476
DENSITY_SCALE = 0.3989422804014327
LANES = 128
SUB = 8
MESH = pl.DeviceIdType.MESH
F32 = jnp.float32
BF16 = jnp.bfloat16
CONTRACT_LAST = (((1,), (1,)), ((), ()))
SMALL_ROWS = 64


def gelu_parts(z):
    bell = jnp.exp(-0.5 * z * z)
    d = 1.0 + (0.3275911 * ROOT_HALF) * jnp.abs(z)
    r = pl.reciprocal(d, approx=True)
    r = r * (2.0 - d * r)
    poly = r * (
        0.127414796
        + r * (-0.142248368 + r * (0.7107068705 + r * (-0.7265760135 + r * 0.5307027145)))
    )
    tail = poly * bell
    cumulative = jnp.where(z >= 0.0, 1.0 - tail, tail)
    return z * cumulative, cumulative + z * (bell * DENSITY_SCALE)


def sizes(inputs_shape, hidden):
    s = types.SimpleNamespace()
    s.L, s.T = lax.axis_size("lon"), lax.axis_size("lat")
    s.R, s.W, s.C = inputs_shape[0], inputs_shape[1] // 2, inputs_shape[2]
    s.M = s.R * s.W
    s.HID = hidden
    s.CB = s.C // LANES
    assert s.CB * 2 == SUB
    s.I0 = 4 * s.CB
    s.WC = s.W * s.CB
    s.COLS = s.WC + 2 * s.I0
    s.ACC = s.WC + SUB
    s.PIECES = s.L * s.T
    s.CHUNK = hidden // s.PIECES
    s.CP = s.C // s.PIECES
    s.BN = max(s.CHUNK, 256)
    s.NB = hidden // s.BN
    s.K = 2 * s.T * s.M
    s.NP = 2 * s.L
    return s


def scratch_of(s):
    dma = pltpu.SemaphoreType.DMA
    vm = pltpu.VMEM
    return dict(
        nat=vm((6, s.R, s.W, s.C), BF16),
        p0=vm((4, s.R + 2 * MARGIN, s.COLS, LANES), F32),
        pb=vm((4, s.R + 2 * MARGIN, s.COLS, LANES), BF16),
        wt=vm((2, KERNEL * KERNEL * SUB, LANES), F32),
        a=vm((2, s.R, s.ACC, LANES), F32),
        ag=vm((2, s.R, s.ACC, LANES), F32),
        kg=vm((KERNEL * KERNEL * SUB, LANES), F32),
        tp=vm((2, KERNEL * KERNEL, s.C), BF16),
        vec=vm((2, 5, 1, s.C), F32),
        hbi=vm((2, 1, s.HID), F32),
        upw=vm((2, s.C, s.HID), BF16),
        dnw=vm((2, s.HID, s.C), BF16),
        un=vm((2, s.M, s.C), F32),
        inv=vm((2, s.M, LANES), F32),
        br=vm((2, s.M, s.C), F32),
        ng=vm((s.M, s.C), F32),
        sl=vm((2, s.NB, s.M, s.BN), F32),
        nrm=vm((s.M, s.C), BF16),
        scl=vm((2, s.M, s.C), BF16),
        hs=vm((2, s.T, s.L, s.M, s.CHUNK), BF16),
        bs=vm((2, s.T, s.L, s.M, s.CHUNK), BF16),
        nts=vm((2, s.C, s.M), BF16),
        sts=vm((2, s.C, s.M), BF16),
        hr=vm((s.L, s.K, s.CHUNK), BF16),
        bgr=vm((s.L, s.K, s.CHUNK), BF16),
        nr=vm((s.C, s.K), BF16),
        sr=vm((s.C, s.K), BF16),
        zs=vm((2, s.L, s.C, s.CHUNK), BF16),
        zr=vm((2, s.L, s.C, s.CHUNK), BF16),
        zo=vm((2, s.C, s.CHUNK), F32),
        vs=vm((2, 5, 1, s.C), F32),
        sm=vm((2, SMALL_ROWS, s.C), F32),
        bh=vm((2, 1, s.HID), F32),
        sc=vm((2, s.PIECES, SMALL_ROWS, s.CP), BF16),
        scr=vm((2 * s.PIECES, SMALL_ROWS, s.CP), BF16),
        load=dma((4,)),
        prm_l=dma((9,)),
        prm_s=dma((9,)),
        prm_r=dma((9,)),
        halo_s=dma((4, 8)),
        halo_r=dma((4, 8)),
        f_s=dma((2, 4, s.T)),
        f_r=dma((4, 2 * s.T)),
        z_s=dma((2, s.L)),
        z_r=dma((2, s.L)),
        s_s=dma((2, s.PIECES)),
        s_r=dma((2 * s.PIECES,)),
        o_s=dma((2, 2)),
        o_r=dma((2,)),
    )


def body(s, names, *refs):
    (x_in, g_in, k_in, cb_in, gain_in, shift_in, up_in, hb_in, dn_in, ob_in, ls_in) = refs[:11]
    so_out, bg_out, up_out, dn_out, hb_out, kg_out, vg_out = refs[11:18]
    v = types.SimpleNamespace(**dict(zip(names, refs[18:])))
    R, W, C, M, L, T, NP, CB = s.R, s.W, s.C, s.M, s.L, s.T, s.NP, s.CB
    c = lax.axis_index("segment")
    l = lax.axis_index("lon")
    t = lax.axis_index("lat")
    p = 2 * l + c
    north = t == 0
    south = t == T - 1

    def cell_at(place, row):
        return {"lat": row, "lon": place // 2, "segment": place % 2}

    def turn(place):
        return (place + NP) % NP

    own_cols = pl.ds(pl.multiple_of(c * W, W), W)
    load_x = pltpu.make_async_copy(x_in.at[:, own_cols, :], v.nat.at[0], v.load.at[0])
    load_g = pltpu.make_async_copy(g_in.at[:, own_cols, :], v.nat.at[3], v.load.at[1])
    load_x.start()
    load_g.start()
    params = [
        (k_in.at[0], v.tp.at[c]),
        (cb_in, v.vec.at[c, 0]),
        (gain_in, v.vec.at[c, 1]),
        (shift_in, v.vec.at[c, 2]),
        (ob_in, v.vec.at[c, 3]),
        (ls_in, v.vec.at[c, 4]),
        (hb_in, v.hbi.at[c]),
        (up_in.at[0], v.upw.at[c]),
        (dn_in.at[0], v.dnw.at[c]),
    ]
    local_params = [
        pltpu.make_async_copy(src, dst, v.prm_l.at[i]) for i, (src, dst) in enumerate(params)
    ]
    remote_params = [
        pltpu.make_async_remote_copy(
            src_ref=src,
            dst_ref=dst,
            send_sem=v.prm_s.at[i],
            recv_sem=v.prm_r.at[i],
            device_id={"segment": 1 - c},
            device_id_type=MESH,
        )
        for i, (src, dst) in enumerate(params)
    ]
    for copy in local_params:
        copy.start()

    barrier = pltpu.get_barrier_semaphore()
    for dl in range(L):
        for dt in range(T):
            for dc in range(2):
                if dl or dt or dc:
                    pl.semaphore_signal(
                        barrier,
                        inc=1,
                        device_id={
                            "lat": lax.rem(t + dt, T),
                            "lon": lax.rem(l + dl, L),
                            "segment": lax.rem(c + dc, 2),
                        },
                        device_id_type=MESH,
                    )
    pl.semaphore_wait(barrier, 2 * L * T - 1)

    mid = pl.ds(s.I0, s.WC)
    first_cols, last_cols = pl.ds(s.I0, s.I0), pl.ds(s.WC, s.I0)
    left_pad, right_pad = pl.ds(0, s.I0), pl.ds(s.I0 + s.WC, s.I0)
    top_rows, low_rows, own_rows = pl.ds(0, MARGIN), pl.ds(R + MARGIN, MARGIN), pl.ds(MARGIN, R)
    regions = [
        (top_rows, mid),
        (top_rows, left_pad),
        (top_rows, right_pad),
        (low_rows, mid),
        (low_rows, left_pad),
        (low_rows, right_pad),
        (own_rows, left_pad),
        (own_rows, right_pad),
    ]
    half = NP // 2
    up_t, up_p = jnp.where(north, t, t - 1), jnp.where(north, p + half, p)
    dn_t, dn_p = jnp.where(south, t, t + 1), jnp.where(south, p + half, p)
    up_to, up_region = jnp.where(north, 0, R + MARGIN), jnp.where(north, 0, 3)
    dn_to, dn_region = jnp.where(south, R + MARGIN, 0), jnp.where(south, 3, 0)

    def halo_sends(n):
        head, tail = pl.ds(MARGIN, MARGIN), pl.ds(R, MARGIN)
        up_rows, dn_rows = pl.ds(up_to, MARGIN), pl.ds(dn_to, MARGIN)
        plans = [
            (head, mid, up_rows, mid, up_region, up_p, up_t),
            (tail, mid, dn_rows, mid, dn_region, dn_p, dn_t),
            (own_rows, first_cols, own_rows, right_pad, 7, p - 1, t),
            (own_rows, last_cols, own_rows, left_pad, 6, p + 1, t),
            (head, first_cols, up_rows, right_pad, up_region + 2, up_p - 1, up_t),
            (head, last_cols, up_rows, left_pad, up_region + 1, up_p + 1, up_t),
            (tail, first_cols, dn_rows, right_pad, dn_region + 2, dn_p - 1, dn_t),
            (tail, last_cols, dn_rows, left_pad, dn_region + 1, dn_p + 1, dn_t),
        ]
        return [
            pltpu.make_async_remote_copy(
                src_ref=v.pb.at[n, rows, cols],
                dst_ref=v.pb.at[n, to_rows, to_cols],
                send_sem=v.halo_s.at[n, i],
                recv_sem=v.halo_r.at[n, region],
                device_id=cell_at(turn(place), row),
                device_id_type=MESH,
            )
            for i, (rows, cols, to_rows, to_cols, region, place, row) in enumerate(plans)
        ]

    def halo_wait(n):
        for g, (rows, cols) in enumerate(regions):
            spot = v.pb.at[n, rows, cols]
            pltpu.make_async_remote_copy(
                src_ref=spot,
                dst_ref=spot,
                send_sem=v.halo_s.at[n, 0],
                recv_sem=v.halo_r.at[n, g],
                device_id={"segment": 1 - c},
                device_id_type=MESH,
            ).wait_recv()
        for a in range(MARGIN):
            up_at = jnp.where(north, MARGIN - 1 - a, a)
            dn_at = R + MARGIN + jnp.where(south, MARGIN - 1 - a, a)
            v.p0[n, up_at] = v.pb[n, a].astype(F32)
            v.p0[n, dn_at] = v.pb[n, R + MARGIN + a].astype(F32)

        def sides(i, carry):
            v.p0[n, i, left_pad] = v.pb[n, i, left_pad].astype(F32)
            v.p0[n, i, right_pad] = v.pb[n, i, right_pad].astype(F32)
            return carry

        lax.fori_loop(MARGIN, R + MARGIN, sides, 0)

    def write_row(n, i, value):
        row = i + MARGIN
        for b in range(CB):
            v.p0[n, row, pl.ds(s.I0 + b, W, stride=CB), :] = value[:, b * LANES : (b + 1) * LANES]
        v.pb[n, row, mid] = v.p0[n, row, mid].astype(BF16)

    def correlate(n, sec, backward):
        def weight(index):
            return v.wt[sec, pl.ds(pl.multiple_of(index * SUB, SUB), SUB), :]

        for parity in range(2):
            col_taps = range(1 - parity, KERNEL, 2)

            def step(k, carry):
                total = jnp.zeros((R, SUB, LANES), F32)
                for q in col_taps:
                    at = pl.multiple_of(SUB * k + SUB * ((q + 1) // 2), SUB)
                    rows = v.p0[n, :, pl.ds(at, SUB), :]
                    for r in range(KERNEL):
                        if backward:
                            index = KERNEL * KERNEL - 1 - (KERNEL * r + q)
                        else:
                            index = KERNEL * r + q
                        w = weight(index)
                        window = rows[r : r + R]
                        if backward and r != MARGIN:
                            edge = KERNEL * r + KERNEL - 1 - q
                            if r < MARGIN:
                                cut = MARGIN - r
                                other = weight(jnp.where(north, edge, index))
                                term = jnp.concatenate(
                                    [window[:cut] * other, window[cut:] * w], axis=0
                                )
                            else:
                                cut = R - (r - MARGIN)
                                other = weight(jnp.where(south, edge, index))
                                term = jnp.concatenate(
                                    [window[:cut] * w, window[cut:] * other], axis=0
                                )
                        else:
                            term = window * w
                        total = total + term
                v.a[parity, :, pl.ds(pl.multiple_of(SUB * k, SUB), SUB), :] = total
                return carry

            lax.fori_loop(0, s.WC // SUB + parity, step, 0)

    def correlated(i):
        return jnp.concatenate(
            [
                v.a[0, i, pl.ds(b, W, stride=CB), :] + v.a[1, i, pl.ds(CB + b, W, stride=CB), :]
                for b in range(CB)
            ],
            axis=1,
        )

    def stencil(n, sec):
        for q in range(KERNEL):
            parity = 1 - q % 2

            def step(k, totals):
                grad = v.ag[parity, :, pl.ds(pl.multiple_of(SUB * k, SUB), SUB), :]
                at = pl.multiple_of(SUB * k + SUB * ((q + 1) // 2), SUB)
                rows = v.p0[n, :, pl.ds(at, SUB), :]
                return tuple(
                    totals[r] + jnp.sum(rows[r : r + R] * grad, axis=0) for r in range(KERNEL)
                )

            zero = jnp.zeros((SUB, LANES), F32)
            totals = lax.fori_loop(0, s.WC // SUB + parity, step, (zero,) * KERNEL)
            for r in range(KERNEL):
                v.kg[pl.ds((KERNEL * r + q) * SUB, SUB), :] = totals[r]
        count = KERNEL * KERNEL
        for b in range(CB):
            v.sm[sec, 0:count, b * LANES : (b + 1) * LANES] = (
                v.kg[pl.ds(b, count, stride=SUB), :] + v.kg[pl.ds(CB + b, count, stride=SUB), :]
            )

    place_k = pl.ds(pl.multiple_of((t * 2 + c) * M, M), M)

    def factor(kind, sec, dt):
        row = lax.rem(t + dt, T)
        if kind == 0:
            return v.hs.at[sec, row], v.hr.at[:, place_k, :]
        if kind == 1:
            return v.bs.at[sec, row], v.bgr.at[:, place_k, :]
        if kind == 2:
            return v.nts.at[sec], v.nr.at[:, place_k]
        return v.sts.at[sec], v.sr.at[:, place_k]

    def factor_remote(kind, sec, dt):
        src, dst = factor(kind, sec, dt)
        return pltpu.make_async_remote_copy(
            src_ref=src,
            dst_ref=dst,
            send_sem=v.f_s.at[sec, kind, dt],
            recv_sem=v.f_r.at[kind, t * 2 + c],
            device_id={"lat": lax.rem(t + dt, T), "segment": sec},
            device_id_type=MESH,
        )

    def factor_local(kind, sec):
        src, dst = factor(kind, sec, 0)
        return pltpu.make_async_copy(src, dst, v.f_r.at[kind, t * 2 + c])

    def send_factor(kind, sec):
        for dt in range(1, T):
            factor_remote(kind, sec, dt).start()

        @pl.when(c == sec)
        def _():
            factor_local(kind, sec).start()

        @pl.when(c != sec)
        def _():
            factor_remote(kind, sec, 0).start()

    def factor_done(kind, sec):
        for dt in range(1, T):
            factor_remote(kind, sec, dt).wait_send()

        @pl.when(c != sec)
        def _():
            factor_remote(kind, sec, 0).wait_send()

    def factor_wait(kind):
        for d in range(2 * T):
            cols = pl.ds(d * M, M)
            spot = [
                v.hr.at[:, cols, :],
                v.bgr.at[:, cols, :],
                v.nr.at[:, cols],
                v.sr.at[:, cols],
            ][kind]
            pltpu.make_async_copy(spot, spot, v.f_r.at[kind, d]).wait()

    def z_copy(mat, i):
        return pltpu.make_async_remote_copy(
            src_ref=v.zs.at[mat, i],
            dst_ref=v.zr.at[mat, i],
            send_sem=v.z_s.at[mat, i],
            recv_sem=v.z_r.at[mat, i],
            device_id={"lon": lax.rem(l + L // 2 + i, L)},
            device_id_type=MESH,
        )

    z_own = L - L // 2

    def dense(sec, mat):
        @pl.when(c == sec)
        def _():
            left, right = (v.sr, v.hr) if mat == 0 else (v.nr, v.bgr)
            factor_wait(3 if mat == 0 else 2)
            factor_wait(0 if mat == 0 else 1)
            for i in range(L):
                to = lax.rem(l + L // 2 + i, L)
                term = jnp.dot(left[...], right[to], preferred_element_type=F32)
                if i == z_own:
                    v.zo[mat] = term
                else:
                    v.zs[mat, i] = term.astype(BF16)
                    z_copy(mat, i).start()

    def z_total(mat):
        total = v.zo[mat]
        for i in range(L):
            if i != z_own:
                z_copy(mat, i).wait_recv()
                total = total + v.zr[mat, i].astype(F32)
        return total

    def small_remote(sec, dl, dt):
        to_l, to_t = lax.rem(l + dl, L), lax.rem(t + dt, T)
        return pltpu.make_async_remote_copy(
            src_ref=v.sc.at[sec, to_l * T + to_t],
            dst_ref=v.scr.at[(dl * T + dt) * 2 + c],
            send_sem=v.s_s.at[sec, dl * T + dt],
            recv_sem=v.s_r.at[(dl * T + dt) * 2 + c],
            device_id={"lat": to_t, "lon": to_l, "segment": sec},
            device_id_type=MESH,
        )

    def small_local(sec):
        return pltpu.make_async_copy(v.sc.at[sec, l * T + t], v.scr.at[c], v.s_r.at[c])

    taps = KERNEL * KERNEL
    bias_rows = s.HID // C

    def send_small(sec):
        for i in range(5):
            v.sm[sec, taps + i : taps + i + 1, :] = v.vs[sec, i]
        for piece in range(s.PIECES):
            v.sc[sec, piece] = v.sm[sec, :, piece * s.CP : (piece + 1) * s.CP].astype(BF16)
            rows = jnp.concatenate(
                [
                    v.bh[sec, :, piece * s.CHUNK + j * s.CP : piece * s.CHUNK + (j + 1) * s.CP]
                    for j in range(bias_rows)
                ]
                + [jnp.zeros((SUB - bias_rows, s.CP), F32)],
                axis=0,
            )
            tail = jnp.concatenate([jnp.zeros((SUB, s.CP), F32), rows], axis=0)
            v.sc[sec, piece, SMALL_ROWS - 2 * SUB : SMALL_ROWS] = (
                v.sm[sec, SMALL_ROWS - 2 * SUB :, piece * s.CP : (piece + 1) * s.CP] + tail
            ).astype(BF16)
        for dl in range(L):
            for dt in range(T):
                if dl or dt:
                    small_remote(sec, dl, dt).start()

        @pl.when(c == sec)
        def _():
            small_local(sec).start()

        @pl.when(c != sec)
        def _():
            small_remote(sec, 0, 0).start()

    def small_done(sec):
        for dl in range(L):
            for dt in range(T):
                if dl or dt:
                    small_remote(sec, dl, dt).wait_send()

        @pl.when(c != sec)
        def _():
            small_remote(sec, 0, 0).wait_send()

    def out_remote(kind, sec, source):
        out = so_out if kind == 0 else bg_out
        return pltpu.make_async_remote_copy(
            src_ref=source,
            dst_ref=out.at[:, own_cols, :],
            send_sem=v.o_s.at[kind, 1],
            recv_sem=v.o_r.at[kind],
            device_id={"segment": sec},
            device_id_type=MESH,
        )

    def out_local(kind, source):
        out = so_out if kind == 0 else bg_out
        return pltpu.make_async_copy(source, out.at[:, own_cols, :], v.o_s.at[kind, 0])

    def send_out(kind, sec, source):
        @pl.when(c == sec)
        def _():
            out_local(kind, source).start()

        @pl.when(c != sec)
        def _():
            out_remote(kind, sec, source).start()

    def vector(sec, which):
        return v.vec[sec, which]

    def wait_param(i, sec):
        @pl.when(c == sec)
        def _():
            local_params[i].wait()

        @pl.when(c != sec)
        def _():
            src, _ = params[i]
            spot = [v.tp.at[sec]] + [v.vec.at[sec, j] for j in range(5)]
            spot = (spot + [v.hbi.at[sec], v.upw.at[sec], v.dnw.at[sec]])[i]
            pltpu.make_async_remote_copy(
                src_ref=spot,
                dst_ref=spot,
                send_sem=v.prm_s.at[i],
                recv_sem=v.prm_r.at[i],
                device_id={"segment": 1 - c},
                device_id_type=MESH,
            ).wait_recv()

    STEP = 2
    CELLS = STEP * W

    def block(ref, i):
        return jnp.concatenate([ref[i * STEP + j] for j in range(STEP)], axis=0)

    def cells(i):
        return pl.ds(pl.multiple_of(i * CELLS, CELLS), CELLS)

    def transpose_into(target, source):
        for b in range(CB):
            piece = source[:, b * LANES : (b + 1) * LANES].astype(F32)
            target[b * LANES : (b + 1) * LANES, :] = piece.T.astype(BF16)

    per = s.BN // s.CHUNK

    def scatter_pieces(ref, sec, b, value):
        for j in range(per):
            index = b * per + j
            ref[sec, lax.rem(index, T), index // T] = value[:, j * s.CHUNK : (j + 1) * s.CHUNK]

    def columns(b):
        return pl.ds(pl.multiple_of(b * s.BN, s.BN), s.BN)

    def forward(sec):
        correlate(sec, sec, False)

        def norm(i, carry):
            x = jnp.concatenate([correlated(i * STEP + j) for j in range(STEP)], axis=0)
            x = x + vector(sec, 0)
            mean = jnp.sum(x, axis=-1, keepdims=True) * (1.0 / C)
            x = x - mean
            var = jnp.sum(x * x, axis=-1, keepdims=True) * (1.0 / C)
            inv = lax.rsqrt(var + EPSILON)
            unit = x * inv
            v.un[sec, cells(i), :] = unit
            v.inv[sec, cells(i), :] = jnp.broadcast_to(inv, (CELLS, LANES))
            v.nrm[cells(i), :] = (unit * vector(sec, 1) + vector(sec, 2)).astype(BF16)
            return carry

        lax.fori_loop(0, R // STEP, norm, 0)
        if sec == 0:
            wait_param(7, sec)
        v.br[sec] = jnp.broadcast_to(vector(sec, 3), (M, C))
        if sec == 0:
            wait_param(8, sec)

        def hidden_block(b, carry):
            before = (
                jnp.dot(v.nrm[...], v.upw[sec, :, columns(b)], preferred_element_type=F32)
                + v.hbi[sec, :, columns(b)]
            )
            active, slope = gelu_parts(before)
            v.sl[sec, b] = slope
            active = active.astype(BF16)
            scatter_pieces(v.hs, sec, b, active)
            v.br[sec] += jnp.dot(active, v.dnw[sec, columns(b), :], preferred_element_type=F32)
            return carry

        lax.fori_loop(0, s.NB, hidden_block, 0)

        def finish(i, carry):
            u = block(v.nat.at[sec], i).astype(F32)
            u = (u + vector(sec, 4) * v.br[sec, cells(i), :]).astype(BF16)
            for j in range(STEP):
                row = u[j * W : (j + 1) * W]
                v.nat[sec + 1, i * STEP + j] = row
                if sec == 0:
                    write_row(1, i * STEP + j, row.astype(F32))
            return carry

        lax.fori_loop(0, R // STEP, finish, 0)

    def scale(sec, at):
        def rows(i, carry):
            g = block(v.nat.at[at], i).astype(F32)
            low = (g * vector(sec, 4)).astype(BF16)
            v.scl[sec, cells(i), :] = low
            return carry + jnp.sum(low.astype(F32), axis=0, keepdims=True)

        v.vs[sec, 3] = lax.fori_loop(0, R // STEP, rows, jnp.zeros((1, C), F32))
        transpose_into(v.sts.at[sec], v.scl.at[sec])

    def branch_sum(sec, at):
        def rows(i, carry):
            g = block(v.nat.at[at], i).astype(F32)
            return carry + jnp.sum(g * v.br[sec, cells(i), :], axis=0, keepdims=True)

        v.vs[sec, 4] = lax.fori_loop(0, R // STEP, rows, jnp.zeros((1, C), F32))

    def backward(sec, n):
        v.ng[...] = jnp.zeros((M, C), F32)

        def hidden_block(b, carry):
            grad = lax.dot_general(
                v.scl[sec], v.dnw[sec, columns(b), :], CONTRACT_LAST, preferred_element_type=F32
            )
            low = (grad * v.sl[sec, b]).astype(BF16)
            scatter_pieces(v.bs, sec, b, low)
            v.bh[sec, :, columns(b)] = jnp.sum(low.astype(F32), axis=0, keepdims=True)
            v.ng[...] += lax.dot_general(
                low, v.upw[sec, :, columns(b)], CONTRACT_LAST, preferred_element_type=F32
            )
            return carry

        lax.fori_loop(0, s.NB, hidden_block, 0)

        def norm(i, carry):
            bias_sum, gain_sum, shift_sum = carry
            ng = v.ng[cells(i), :]
            unit = v.un[sec, cells(i), :]
            inv = v.inv[sec, cells(i), :][:, :1]
            both = ng * unit
            gained = ng * vector(sec, 1)
            mean = jnp.sum(gained, axis=-1, keepdims=True) * (1.0 / C)
            along = jnp.sum(gained * unit, axis=-1, keepdims=True) * (1.0 / C)
            grad = (inv * (gained - mean - unit * along)).astype(BF16).astype(F32)
            for j in range(STEP):
                row = grad[j * W : (j + 1) * W]
                write_row(n, i * STEP + j, row)
                for b in range(CB):
                    lanes = row[:, b * LANES : (b + 1) * LANES]
                    v.ag[0, i * STEP + j, pl.ds(b, W, stride=CB), :] = lanes
                    v.ag[1, i * STEP + j, pl.ds(CB + b, W, stride=CB), :] = lanes
            return (
                bias_sum + jnp.sum(grad, axis=0, keepdims=True),
                gain_sum + jnp.sum(both, axis=0, keepdims=True),
                shift_sum + jnp.sum(ng, axis=0, keepdims=True),
            )

        zero = jnp.zeros((1, C), F32)
        totals = lax.fori_loop(0, R // STEP, norm, (zero, zero, zero))
        for i in range(3):
            v.vs[sec, i] = totals[i]

    def through(sec, n, at, to):
        correlate(n, sec, True)

        def rows(i, carry):
            g = v.nat[at, i].astype(F32)
            v.nat[to, i] = (g + correlated(i)).astype(BF16)
            return carry

        lax.fori_loop(0, R, rows, 0)

    for copy in remote_params:
        copy.start()
    load_x.wait()

    def first_rows(i, carry):
        write_row(0, i, v.nat[0, i].astype(F32))
        return carry

    lax.fori_loop(0, R, first_rows, 0)
    for copy in halo_sends(0):
        copy.start()
    for sec in range(2):
        for i in range(7):
            wait_param(i, sec)
        for b in range(CB):
            piece = v.tp[sec, :, b * LANES : (b + 1) * LANES].astype(F32)
            v.wt[sec, pl.ds(b, taps, stride=SUB), :] = piece
            v.wt[sec, pl.ds(CB + b, taps, stride=SUB), :] = piece
    for sec in range(2):
        v.sm[sec] = jnp.zeros((SMALL_ROWS, C), F32)
    for i in range(R):
        v.ag[0, i, s.WC : s.ACC] = jnp.zeros((SUB, LANES), F32)
        v.ag[1, i, 0:SUB] = jnp.zeros((SUB, LANES), F32)
        v.ag[1, i, s.WC : s.ACC] = jnp.zeros((SUB, LANES), F32)
    load_g.wait()
    scale(1, 3)
    send_factor(3, 1)

    halo_wait(0)
    forward(0)
    for copy in halo_sends(1):
        copy.start()
    transpose_into(v.nts.at[0], v.nrm)
    send_factor(0, 0)
    send_factor(2, 0)
    send_out(0, 0, v.nat.at[1])
    wait_param(7, 1)
    wait_param(8, 1)

    halo_wait(1)
    forward(1)
    send_factor(0, 1)
    transpose_into(v.nts.at[1], v.nrm)
    send_factor(2, 1)
    send_out(0, 1, v.nat.at[2])
    backward(1, 2)
    for copy in halo_sends(2):
        copy.start()
    send_factor(1, 1)
    branch_sum(1, 3)
    dense(1, 0)
    stencil(1, 1)
    send_small(1)

    halo_wait(2)
    through(1, 2, 3, 4)
    send_out(1, 1, v.nat.at[4])
    scale(0, 4)
    send_factor(3, 0)
    backward(0, 3)
    for copy in halo_sends(3):
        copy.start()
    send_factor(1, 0)
    branch_sum(0, 4)
    dense(1, 1)
    dense(0, 0)
    stencil(0, 0)
    send_small(0)
    dense(0, 1)

    halo_wait(3)
    through(0, 3, 4, 5)
    send_out(1, 0, v.nat.at[5])

    total = jnp.zeros((SMALL_ROWS, s.CP), F32)
    for i in range(2 * s.PIECES):
        pltpu.make_async_copy(v.scr.at[i], v.scr.at[i], v.s_r.at[i]).wait()
        total = total + v.scr[i].astype(F32)
    kg_out[...] = total[:taps]
    vg_out[...] = total[taps : taps + 5]
    for j in range(bias_rows):
        row = SMALL_ROWS - SUB + j
        hb_out[:, j * s.CP : (j + 1) * s.CP] = total[row : row + 1]
    dn_out[...] = z_total(0).T
    up_out[...] = z_total(1)

    for kind in range(2):
        source = v.nat.at[0]

        @pl.when(c == 0)
        def _():
            out_remote(kind, 1, source).wait_send()
            out_local(kind, source).wait()

        @pl.when(c == 1)
        def _():
            out_remote(kind, 0, source).wait_send()
            out_local(kind, source).wait()

        out = so_out if kind == 0 else bg_out
        spot = out.at[:, pl.ds(pl.multiple_of((1 - c) * W, W), W), :]
        pltpu.make_async_remote_copy(
            src_ref=spot,
            dst_ref=spot,
            send_sem=v.o_s.at[kind, 1],
            recv_sem=v.o_r.at[kind],
            device_id={"segment": 1 - c},
            device_id_type=MESH,
        ).wait_recv()
    for copy in remote_params:
        copy.wait_send()
    for n in range(4):
        for copy in halo_sends(n):
            copy.wait_send()
    for sec in range(2):
        for kind in range(4):
            factor_done(kind, sec)
        small_done(sec)
    for mat in range(2):
        for i in range(L):
            if i != z_own:
                z_copy(mat, i).wait_send()


def local(*args):
    inputs, up_weight = args[0], args[6]
    s = sizes(inputs.shape, up_weight.shape[2])
    scratch = scratch_of(s)
    full = pl.BlockSpec(memory_space=pltpu.VMEM)
    hbm = pl.BlockSpec(memory_space=pl.ANY)
    section_out, boundary_grad, up_grad, down_grad, bias_grad, kernel_grad, vector_grad = (
        pl.pallas_call(
            functools.partial(body, s, tuple(scratch)),
            out_shape=[
                jax.ShapeDtypeStruct(inputs.shape, BF16),
                jax.ShapeDtypeStruct(inputs.shape, BF16),
                jax.ShapeDtypeStruct((s.C, s.CHUNK), F32),
                jax.ShapeDtypeStruct((s.CHUNK, s.C), F32),
                jax.ShapeDtypeStruct((1, s.CHUNK), F32),
                jax.ShapeDtypeStruct((KERNEL * KERNEL, s.CP), F32),
                jax.ShapeDtypeStruct((5, s.CP), F32),
            ],
            in_specs=[hbm] * len(args),
            out_specs=[hbm, hbm] + [full] * 5,
            scratch_shapes=list(scratch.values()),
            compiler_params=pltpu.CompilerParams(
                collective_id=0, has_side_effects=True, vmem_limit_bytes=58 * 1024 * 1024
            ),
        )(*args)
    )
    return (
        section_out[None],
        boundary_grad[None],
        up_grad[None],
        down_grad[None],
        bias_grad,
        kernel_grad[None],
        vector_grad[None],
    )


def solution(mesh):
    placed = (
        P(("groups", "lat"), "lon", None),
        P(("groups", "lat"), "lon", None),
        P("segment", None, None),
        P("segment", None),
        P("segment", None),
        P("segment", None),
        P("segment", None, None),
        P("segment", None),
        P("segment", None, None),
        P("segment", None),
        P("segment", None),
    )
    return jax.shard_map(
        local,
        mesh=mesh,
        in_specs=placed,
        out_specs=(
            P("segment", ("groups", "lat"), "lon", None),
            P("segment", ("groups", "lat"), "lon", None),
            P(("groups", "segment"), None, ("lon", "lat")),
            P(("groups", "segment"), ("lon", "lat"), None),
            P(("groups", "segment"), ("lon", "lat")),
            P(("groups", "segment"), None, ("lon", "lat")),
            P(("groups", "segment"), None, ("lon", "lat")),
        ),
        check_vma=False,
    )
```

```python
import functools
import types
import jax
import jax.numpy as jnp
from jax import lax
from jax.experimental import pallas as pl
from jax.experimental.pallas import tpu as pltpu
from jax.sharding import PartitionSpec as P

KERNEL = 7
MARGIN = KERNEL // 2
EPSILON = 1e-06
ROOT_HALF = 0.7071067811865476
DENSITY_SCALE = 0.3989422804014327
LANES = 128
SUB = 8
MESH = pl.DeviceIdType.MESH
F32 = jnp.float32
BF16 = jnp.bfloat16
CONTRACT_LAST = (((1,), (1,)), ((), ()))
SMALL_ROWS = 64
HALVES = 1


def gelu_parts(z):
    bell = jnp.exp(-0.5 * z * z)
    d = 1.0 + (0.3275911 * ROOT_HALF) * jnp.abs(z)
    r = pl.reciprocal(d, approx=True)
    r = r * (2.0 - d * r)
    poly = r * (
        0.127414796
        + r * (-0.142248368 + r * (0.7107068705 + r * (-0.7265760135 + r * 0.5307027145)))
    )
    tail = poly * bell
    cumulative = jnp.where(z >= 0.0, 1.0 - tail, tail)
    return z * cumulative, cumulative + z * (bell * DENSITY_SCALE)


def sizes(inputs_shape, hidden):
    s = types.SimpleNamespace()
    s.L, s.T = lax.axis_size("lon"), lax.axis_size("lat")
    s.R, s.W, s.C = inputs_shape[0], inputs_shape[1] // 2, inputs_shape[2]
    s.M = s.R * s.W
    s.HID = hidden
    s.CB = s.C // LANES
    assert s.CB * 2 == SUB
    s.I0 = 4 * s.CB
    s.WC = s.W * s.CB
    s.COLS = s.WC + 2 * s.I0
    s.ACC = s.WC + SUB
    s.PIECES = s.L * s.T
    s.CHUNK = hidden // s.PIECES
    s.CP = s.C // s.PIECES
    s.BN = max(s.CHUNK, 256)
    s.NB = hidden // s.BN
    s.K = 2 * s.T * s.M
    s.NP = 2 * s.L
    return s


def scratch_of(s):
    dma = pltpu.SemaphoreType.DMA
    vm = pltpu.VMEM
    return dict(
        nat=vm((6, s.R, s.W, s.C), BF16),
        p0=vm((4, s.R + 2 * MARGIN, s.COLS, LANES), F32),
        pb=vm((4, s.R + 2 * MARGIN, s.COLS, LANES), BF16),
        wt=vm((2, KERNEL * KERNEL * SUB, LANES), F32),
        a=vm((2, s.R, s.ACC, LANES), F32),
        ag=vm((2, s.R, s.ACC, LANES), F32),
        kg=vm((KERNEL * KERNEL * SUB, LANES), F32),
        tp=vm((2, KERNEL * KERNEL, s.C), BF16),
        vec=vm((2, 5, 1, s.C), F32),
        hbi=vm((2, 1, s.HID), F32),
        upw=vm((2, s.C, s.HID), BF16),
        dnw=vm((2, s.HID, s.C), BF16),
        un=vm((2, s.M, s.C), F32),
        inv=vm((2, s.M, LANES), F32),
        br=vm((2, s.M, s.C), F32),
        ng=vm((s.M, s.C), F32),
        sl=vm((2, s.NB, s.M, s.BN), F32),
        nrm=vm((s.M, s.C), BF16),
        scl=vm((2, s.M, s.C), BF16),
        hs=vm((2, s.T, s.L, s.M, s.CHUNK), BF16),
        bs=vm((2, s.T, s.L, s.M, s.CHUNK), BF16),
        nts=vm((2, s.C, s.M), BF16),
        sts=vm((2, s.C, s.M), BF16),
        hr=vm((s.L, s.K, s.CHUNK), BF16),
        bgr=vm((s.L, s.K, s.CHUNK), BF16),
        nr=vm((2 * s.T, s.C, s.M), BF16),
        sr=vm((2 * s.T, s.C, s.M), BF16),
        zs=vm((2, s.L, s.C, s.CHUNK), BF16),
        zm=vm((2, s.L, s.C, s.CHUNK), BF16),
        zr=vm((2, s.L // 2, s.C, s.CHUNK), BF16),
        zo=vm((2, s.C, s.CHUNK), F32),
        vs=vm((2, 5, 1, s.C), F32),
        sm=vm((2, SMALL_ROWS, s.C), F32),
        bh=vm((2, 1, s.HID), F32),
        sc=vm((2, s.PIECES, SMALL_ROWS, s.CP), BF16),
        scr=vm((2 * s.PIECES, SMALL_ROWS, s.CP), BF16),
        load=dma((4,)),
        prm_l=dma((7 + 2 * HALVES,)),
        prm_s=dma((7 + 2 * HALVES,)),
        prm_r=dma((7 + 2 * HALVES,)),
        halo_s=dma((4, 8)),
        halo_r=dma((4, 8)),
        f_s=dma((2, 4, s.T, s.L)),
        f_r=dma((4, 2 * s.T, s.L)),
        z_s=dma((2, s.L)),
        zm_r=dma((2, s.L)),
        z_r=dma((2, s.L // 2)),
        s_s=dma((2, s.PIECES)),
        s_r=dma((2 * s.PIECES,)),
        o_s=dma((2, 2)),
        o_r=dma((2,)),
    )


def body(s, names, *refs):
    (x_in, g_in, k_in, cb_in, gain_in, shift_in, up_in, hb_in, dn_in, ob_in, ls_in) = refs[:11]
    so_out, bg_out, up_out, dn_out, hb_out, kg_out, vg_out = refs[11:18]
    v = types.SimpleNamespace(**dict(zip(names, refs[18:])))
    R, W, C, M, L, T, NP, CB = s.R, s.W, s.C, s.M, s.L, s.T, s.NP, s.CB
    c = lax.axis_index("segment")
    l = lax.axis_index("lon")
    t = lax.axis_index("lat")
    p = 2 * l + c
    north = t == 0
    south = t == T - 1

    def cell_at(place, row):
        return {"lat": row, "lon": place // 2, "segment": place % 2}

    def turn(place):
        return (place + NP) % NP

    own_cols = pl.ds(pl.multiple_of(c * W, W), W)
    load_x = pltpu.make_async_copy(x_in.at[:, own_cols, :], v.nat.at[0], v.load.at[0])
    load_g = pltpu.make_async_copy(g_in.at[:, own_cols, :], v.nat.at[3], v.load.at[1])
    load_x.start()
    load_g.start()
    params = [
        (k_in.at[0], v.tp.at[c]),
        (cb_in, v.vec.at[c, 0]),
        (gain_in, v.vec.at[c, 1]),
        (shift_in, v.vec.at[c, 2]),
        (ob_in, v.vec.at[c, 3]),
        (ls_in, v.vec.at[c, 4]),
        (hb_in, v.hbi.at[c]),
    ]
    width = s.HID // HALVES
    for h in range(HALVES):
        cols = pl.ds(h * width, width)
        params.append((up_in.at[0, :, cols], v.upw.at[c, :, cols]))
        params.append((dn_in.at[0, cols, :], v.dnw.at[c, cols, :]))
    local_params = [
        pltpu.make_async_copy(src, dst, v.prm_l.at[i]) for i, (src, dst) in enumerate(params)
    ]
    remote_params = [
        pltpu.make_async_remote_copy(
            src_ref=src,
            dst_ref=dst,
            send_sem=v.prm_s.at[i],
            recv_sem=v.prm_r.at[i],
            device_id={"segment": 1 - c},
            device_id_type=MESH,
        )
        for i, (src, dst) in enumerate(params)
    ]
    for copy in local_params:
        copy.start()

    barrier = pltpu.get_barrier_semaphore()
    for dl in range(L):
        for dt in range(T):
            for dc in range(2):
                if dl or dt or dc:
                    pl.semaphore_signal(
                        barrier,
                        inc=1,
                        device_id={
                            "lat": lax.rem(t + dt, T),
                            "lon": lax.rem(l + dl, L),
                            "segment": lax.rem(c + dc, 2),
                        },
                        device_id_type=MESH,
                    )
    pl.semaphore_wait(barrier, 2 * L * T - 1)

    mid = pl.ds(s.I0, s.WC)
    first_cols, last_cols = pl.ds(s.I0, s.I0), pl.ds(s.WC, s.I0)
    left_pad, right_pad = pl.ds(0, s.I0), pl.ds(s.I0 + s.WC, s.I0)
    top_rows, low_rows, own_rows = pl.ds(0, MARGIN), pl.ds(R + MARGIN, MARGIN), pl.ds(MARGIN, R)
    regions = [
        (top_rows, mid),
        (top_rows, left_pad),
        (top_rows, right_pad),
        (low_rows, mid),
        (low_rows, left_pad),
        (low_rows, right_pad),
        (own_rows, left_pad),
        (own_rows, right_pad),
    ]
    half = NP // 2
    up_t, up_p = jnp.where(north, t, t - 1), jnp.where(north, p + half, p)
    dn_t, dn_p = jnp.where(south, t, t + 1), jnp.where(south, p + half, p)
    up_to, up_region = jnp.where(north, 0, R + MARGIN), jnp.where(north, 0, 3)
    dn_to, dn_region = jnp.where(south, R + MARGIN, 0), jnp.where(south, 3, 0)

    def halo_sends(n):
        head, tail = pl.ds(MARGIN, MARGIN), pl.ds(R, MARGIN)
        up_rows, dn_rows = pl.ds(up_to, MARGIN), pl.ds(dn_to, MARGIN)
        plans = [
            (head, mid, up_rows, mid, up_region, up_p, up_t),
            (tail, mid, dn_rows, mid, dn_region, dn_p, dn_t),
            (own_rows, first_cols, own_rows, right_pad, 7, p - 1, t),
            (own_rows, last_cols, own_rows, left_pad, 6, p + 1, t),
            (head, first_cols, up_rows, right_pad, up_region + 2, up_p - 1, up_t),
            (head, last_cols, up_rows, left_pad, up_region + 1, up_p + 1, up_t),
            (tail, first_cols, dn_rows, right_pad, dn_region + 2, dn_p - 1, dn_t),
            (tail, last_cols, dn_rows, left_pad, dn_region + 1, dn_p + 1, dn_t),
        ]
        return [
            pltpu.make_async_remote_copy(
                src_ref=v.pb.at[n, rows, cols],
                dst_ref=v.pb.at[n, to_rows, to_cols],
                send_sem=v.halo_s.at[n, i],
                recv_sem=v.halo_r.at[n, region],
                device_id=cell_at(turn(place), row),
                device_id_type=MESH,
            )
            for i, (rows, cols, to_rows, to_cols, region, place, row) in enumerate(plans)
        ]

    def halo_wait(n):
        for g, (rows, cols) in enumerate(regions):
            spot = v.pb.at[n, rows, cols]
            pltpu.make_async_remote_copy(
                src_ref=spot,
                dst_ref=spot,
                send_sem=v.halo_s.at[n, 0],
                recv_sem=v.halo_r.at[n, g],
                device_id={"segment": 1 - c},
                device_id_type=MESH,
            ).wait_recv()
        for a in range(MARGIN):
            up_at = jnp.where(north, MARGIN - 1 - a, a)
            dn_at = R + MARGIN + jnp.where(south, MARGIN - 1 - a, a)
            v.p0[n, up_at] = v.pb[n, a].astype(F32)
            v.p0[n, dn_at] = v.pb[n, R + MARGIN + a].astype(F32)

        def sides(i, carry):
            v.p0[n, i, left_pad] = v.pb[n, i, left_pad].astype(F32)
            v.p0[n, i, right_pad] = v.pb[n, i, right_pad].astype(F32)
            return carry

        lax.fori_loop(MARGIN, R + MARGIN, sides, 0)

    def write_row(n, i, value):
        row = i + MARGIN
        for b in range(CB):
            v.p0[n, row, pl.ds(s.I0 + b, W, stride=CB), :] = value[:, b * LANES : (b + 1) * LANES]
        v.pb[n, row, mid] = v.p0[n, row, mid].astype(BF16)

    def correlate(n, sec, backward):
        def weight(index):
            return v.wt[sec, pl.ds(pl.multiple_of(index * SUB, SUB), SUB), :]

        for parity in range(2):
            col_taps = range(1 - parity, KERNEL, 2)

            def step(k, carry):
                total = jnp.zeros((R, SUB, LANES), F32)
                for q in col_taps:
                    at = pl.multiple_of(SUB * k + SUB * ((q + 1) // 2), SUB)
                    rows = v.p0[n, :, pl.ds(at, SUB), :]
                    for r in range(KERNEL):
                        if backward:
                            index = KERNEL * KERNEL - 1 - (KERNEL * r + q)
                        else:
                            index = KERNEL * r + q
                        w = weight(index)
                        window = rows[r : r + R]
                        if backward and r != MARGIN:
                            edge = KERNEL * r + KERNEL - 1 - q
                            if r < MARGIN:
                                cut = MARGIN - r
                                other = weight(jnp.where(north, edge, index))
                                term = jnp.concatenate(
                                    [window[:cut] * other, window[cut:] * w], axis=0
                                )
                            else:
                                cut = R - (r - MARGIN)
                                other = weight(jnp.where(south, edge, index))
                                term = jnp.concatenate(
                                    [window[:cut] * w, window[cut:] * other], axis=0
                                )
                        else:
                            term = window * w
                        total = total + term
                v.a[parity, :, pl.ds(pl.multiple_of(SUB * k, SUB), SUB), :] = total
                return carry

            lax.fori_loop(0, s.WC // SUB + parity, step, 0)

    def correlated(i):
        return jnp.concatenate(
            [
                v.a[0, i, pl.ds(b, W, stride=CB), :] + v.a[1, i, pl.ds(CB + b, W, stride=CB), :]
                for b in range(CB)
            ],
            axis=1,
        )

    def stencil(n, sec):
        for q in range(KERNEL):
            parity = 1 - q % 2

            def step(k, totals):
                grad = v.ag[parity, :, pl.ds(pl.multiple_of(SUB * k, SUB), SUB), :]
                at = pl.multiple_of(SUB * k + SUB * ((q + 1) // 2), SUB)
                rows = v.p0[n, :, pl.ds(at, SUB), :]
                return tuple(
                    totals[r] + jnp.sum(rows[r : r + R] * grad, axis=0) for r in range(KERNEL)
                )

            zero = jnp.zeros((SUB, LANES), F32)
            totals = lax.fori_loop(0, s.WC // SUB + parity, step, (zero,) * KERNEL)
            for r in range(KERNEL):
                v.kg[pl.ds((KERNEL * r + q) * SUB, SUB), :] = totals[r]
        count = KERNEL * KERNEL
        for b in range(CB):
            v.sm[sec, 0:count, b * LANES : (b + 1) * LANES] = (
                v.kg[pl.ds(b, count, stride=SUB), :] + v.kg[pl.ds(CB + b, count, stride=SUB), :]
            )

    source = t * 2 + c
    place_k = pl.ds(pl.multiple_of(source * M, M), M)
    even = lax.rem(l, 2) == 0
    partner = l + 1 - 2 * lax.rem(l, 2)

    def z_to(i):
        to = jnp.where(even, L - 1 - i, i)
        beyond = jnp.where(even, to > l, to < l)
        return to, beyond

    def factor(kind, sec, dt, to):
        row = lax.rem(t + dt, T)
        if kind == 0:
            return v.hs.at[sec, row, to], v.hr.at[to, place_k, :]
        if kind == 1:
            return v.bs.at[sec, row, to], v.bgr.at[to, place_k, :]
        if kind == 2:
            return v.nts.at[sec], v.nr.at[source]
        return v.sts.at[sec], v.sr.at[source]

    def factor_remote(kind, sec, dt, to):
        src, dst = factor(kind, sec, dt, to)
        return pltpu.make_async_remote_copy(
            src_ref=src,
            dst_ref=dst,
            send_sem=v.f_s.at[sec, kind, dt, to],
            recv_sem=v.f_r.at[kind, source, to],
            device_id={"lat": lax.rem(t + dt, T), "segment": sec},
            device_id_type=MESH,
        )

    def factor_local(kind, sec, to):
        src, dst = factor(kind, sec, 0, to)
        return pltpu.make_async_copy(src, dst, v.f_r.at[kind, source, to])

    def send_factor(kind, sec):
        for i in range(L if kind < 2 else 1):
            to = z_to(i)[0] if kind < 2 else 0
            for dt in range(1, T):
                factor_remote(kind, sec, dt, to).start()

            @pl.when(c == sec)
            def _():
                factor_local(kind, sec, to).start()

            @pl.when(c != sec)
            def _():
                factor_remote(kind, sec, 0, to).start()

    def factor_done(kind, sec):
        for to in range(L if kind < 2 else 1):
            for dt in range(1, T):
                factor_remote(kind, sec, dt, to).wait_send()

            @pl.when(c != sec)
            def _():
                factor_remote(kind, sec, 0, to).wait_send()

    def factor_wait(kind, to):
        for d in range(2 * T):
            rows = pl.ds(d * M, M)
            if kind == 0:
                spot = v.hr.at[to, rows, :]
            elif kind == 1:
                spot = v.bgr.at[to, rows, :]
            else:
                spot = (v.nr if kind == 2 else v.sr).at[d]
            pltpu.make_async_copy(spot, spot, v.f_r.at[kind, d, to]).wait()

    def z_merge(mat, to):
        return pltpu.make_async_remote_copy(
            src_ref=v.zs.at[mat, to],
            dst_ref=v.zm.at[mat, to],
            send_sem=v.z_s.at[mat, to],
            recv_sem=v.zm_r.at[mat, to],
            device_id={"lon": partner},
            device_id_type=MESH,
        )

    def z_final(mat, to):
        return pltpu.make_async_remote_copy(
            src_ref=v.zs.at[mat, to],
            dst_ref=v.zr.at[mat, l // 2],
            send_sem=v.z_s.at[mat, to],
            recv_sem=v.z_r.at[mat, l // 2],
            device_id={"lon": to},
            device_id_type=MESH,
        )

    def dense(sec, mat):
        @pl.when(c == sec)
        def _():
            left, right = (v.sr, v.hr) if mat == 0 else (v.nr, v.bgr)
            factor_wait(3 if mat == 0 else 2, 0)
            for i in range(L):
                to, beyond = z_to(i)
                factor_wait(0 if mat == 0 else 1, to)
                wide = jnp.concatenate([left[d] for d in range(2 * T)], axis=1)
                term = jnp.dot(wide, right[to], preferred_element_type=F32)

                @pl.when(beyond)
                def _():
                    v.zs[mat, to] = term.astype(BF16)

                    @pl.when(to == partner)
                    def _():
                        z_final(mat, to).start()

                    @pl.when(to != partner)
                    def _():
                        z_merge(mat, to).start()

                @pl.when(to == l)
                def _():
                    v.zo[mat] = term

                @pl.when(jnp.logical_not(jnp.logical_or(beyond, to == l)))
                def _():
                    v.zs[mat, to] = term.astype(BF16)

    def service(sec, mat):
        @pl.when(c == sec)
        def _():
            for i in range(L):
                to, beyond = z_to(i)

                @pl.when(jnp.logical_and(jnp.logical_not(beyond), to != l))
                def _():
                    z_merge(mat, to).wait_recv()
                    total = v.zs[mat, to].astype(F32) + v.zm[mat, to].astype(F32)
                    v.zs[mat, to] = total.astype(BF16)
                    z_final(mat, to).start()

    def z_total(mat):
        total = v.zo[mat]
        for j in range(L // 2):
            spot = v.zr.at[mat, j]
            pltpu.make_async_copy(spot, spot, v.z_r.at[mat, j]).wait()
            total = total + v.zr[mat, j].astype(F32)
        return total

    def small_remote(sec, dl, dt):
        to_l, to_t = lax.rem(l + dl, L), lax.rem(t + dt, T)
        return pltpu.make_async_remote_copy(
            src_ref=v.sc.at[sec, to_l * T + to_t],
            dst_ref=v.scr.at[(dl * T + dt) * 2 + c],
            send_sem=v.s_s.at[sec, dl * T + dt],
            recv_sem=v.s_r.at[(dl * T + dt) * 2 + c],
            device_id={"lat": to_t, "lon": to_l, "segment": sec},
            device_id_type=MESH,
        )

    def small_local(sec):
        return pltpu.make_async_copy(v.sc.at[sec, l * T + t], v.scr.at[c], v.s_r.at[c])

    taps = KERNEL * KERNEL
    bias_rows = s.HID // C

    def send_small(sec):
        for i in range(5):
            v.sm[sec, taps + i : taps + i + 1, :] = v.vs[sec, i]
        for piece in range(s.PIECES):
            v.sc[sec, piece] = v.sm[sec, :, piece * s.CP : (piece + 1) * s.CP].astype(BF16)
            rows = jnp.concatenate(
                [
                    v.bh[sec, :, piece * s.CHUNK + j * s.CP : piece * s.CHUNK + (j + 1) * s.CP]
                    for j in range(bias_rows)
                ]
                + [jnp.zeros((SUB - bias_rows, s.CP), F32)],
                axis=0,
            )
            tail = jnp.concatenate([jnp.zeros((SUB, s.CP), F32), rows], axis=0)
            v.sc[sec, piece, SMALL_ROWS - 2 * SUB : SMALL_ROWS] = (
                v.sm[sec, SMALL_ROWS - 2 * SUB :, piece * s.CP : (piece + 1) * s.CP] + tail
            ).astype(BF16)
        for dl in range(L):
            for dt in range(T):
                if dl or dt:
                    small_remote(sec, dl, dt).start()

        @pl.when(c == sec)
        def _():
            small_local(sec).start()

        @pl.when(c != sec)
        def _():
            small_remote(sec, 0, 0).start()

    def small_done(sec):
        for dl in range(L):
            for dt in range(T):
                if dl or dt:
                    small_remote(sec, dl, dt).wait_send()

        @pl.when(c != sec)
        def _():
            small_remote(sec, 0, 0).wait_send()

    def out_remote(kind, sec, source):
        out = so_out if kind == 0 else bg_out
        return pltpu.make_async_remote_copy(
            src_ref=source,
            dst_ref=out.at[:, own_cols, :],
            send_sem=v.o_s.at[kind, 1],
            recv_sem=v.o_r.at[kind],
            device_id={"segment": sec},
            device_id_type=MESH,
        )

    def out_local(kind, source):
        out = so_out if kind == 0 else bg_out
        return pltpu.make_async_copy(source, out.at[:, own_cols, :], v.o_s.at[kind, 0])

    def send_out(kind, sec, source):
        @pl.when(c == sec)
        def _():
            out_local(kind, source).start()

        @pl.when(c != sec)
        def _():
            out_remote(kind, sec, source).start()

    def vector(sec, which):
        return v.vec[sec, which]

    def wait_param(i, sec):
        @pl.when(c == sec)
        def _():
            local_params[i].wait()

        @pl.when(c != sec)
        def _():
            src, _ = params[i]
            spot = [v.tp.at[sec]] + [v.vec.at[sec, j] for j in range(5)]
            spot = spot + [v.hbi.at[sec]]
            for h in range(HALVES):
                cols = pl.ds(h * width, width)
                spot = spot + [v.upw.at[sec, :, cols], v.dnw.at[sec, cols, :]]
            spot = spot[i]
            pltpu.make_async_remote_copy(
                src_ref=spot,
                dst_ref=spot,
                send_sem=v.prm_s.at[i],
                recv_sem=v.prm_r.at[i],
                device_id={"segment": 1 - c},
                device_id_type=MESH,
            ).wait_recv()

    STEP = 2
    CELLS = STEP * W

    def block(ref, i):
        return jnp.concatenate([ref[i * STEP + j] for j in range(STEP)], axis=0)

    def cells(i):
        return pl.ds(pl.multiple_of(i * CELLS, CELLS), CELLS)

    def transpose_into(target, source):
        for b in range(CB):
            piece = source[:, b * LANES : (b + 1) * LANES].astype(F32)
            target[b * LANES : (b + 1) * LANES, :] = piece.T.astype(BF16)

    per = s.BN // s.CHUNK

    def scatter_pieces(ref, sec, b, value):
        for j in range(per):
            index = b * per + j
            ref[sec, lax.rem(index, T), index // T] = value[:, j * s.CHUNK : (j + 1) * s.CHUNK]

    def columns(b):
        return pl.ds(pl.multiple_of(b * s.BN, s.BN), s.BN)

    def forward(sec):
        correlate(sec, sec, False)

        def norm(i, carry):
            x = jnp.concatenate([correlated(i * STEP + j) for j in range(STEP)], axis=0)
            x = x + vector(sec, 0)
            mean = jnp.sum(x, axis=-1, keepdims=True) * (1.0 / C)
            x = x - mean
            var = jnp.sum(x * x, axis=-1, keepdims=True) * (1.0 / C)
            inv = lax.rsqrt(var + EPSILON)
            unit = x * inv
            v.un[sec, cells(i), :] = unit
            v.inv[sec, cells(i), :] = jnp.broadcast_to(inv, (CELLS, LANES))
            v.nrm[cells(i), :] = (unit * vector(sec, 1) + vector(sec, 2)).astype(BF16)
            return carry

        lax.fori_loop(0, R // STEP, norm, 0)
        transpose_into(v.nts.at[sec], v.nrm)
        if sec == 1:
            send_factor(2, 1)
        v.br[sec] = jnp.broadcast_to(vector(sec, 3), (M, C))

        def hidden_block(b, carry):
            before = (
                jnp.dot(v.nrm[...], v.upw[sec, :, columns(b)], preferred_element_type=F32)
                + v.hbi[sec, :, columns(b)]
            )
            active, slope = gelu_parts(before)
            v.sl[sec, b] = slope
            active = active.astype(BF16)
            scatter_pieces(v.hs, sec, b, active)
            v.br[sec] += jnp.dot(active, v.dnw[sec, columns(b), :], preferred_element_type=F32)
            return carry

        step = s.NB // HALVES
        for h in range(HALVES):
            wait_param(7 + 2 * h, sec)
            wait_param(8 + 2 * h, sec)
            lax.fori_loop(h * step, (h + 1) * step, hidden_block, 0, unroll=True)

        def finish(i, carry):
            u = block(v.nat.at[sec], i).astype(F32)
            u = (u + vector(sec, 4) * v.br[sec, cells(i), :]).astype(BF16)
            for j in range(STEP):
                row = u[j * W : (j + 1) * W]
                v.nat[sec + 1, i * STEP + j] = row
                if sec == 0:
                    write_row(1, i * STEP + j, row.astype(F32))
            return carry

        lax.fori_loop(0, R // STEP, finish, 0)

    def scale(sec, at):
        def rows(i, carry):
            g = block(v.nat.at[at], i).astype(F32)
            low = (g * vector(sec, 4)).astype(BF16)
            v.scl[sec, cells(i), :] = low
            return carry + jnp.sum(low.astype(F32), axis=0, keepdims=True)

        v.vs[sec, 3] = lax.fori_loop(0, R // STEP, rows, jnp.zeros((1, C), F32))
        transpose_into(v.sts.at[sec], v.scl.at[sec])

    def branch_sum(sec, at):
        def rows(i, carry):
            g = block(v.nat.at[at], i).astype(F32)
            return carry + jnp.sum(g * v.br[sec, cells(i), :], axis=0, keepdims=True)

        v.vs[sec, 4] = lax.fori_loop(0, R // STEP, rows, jnp.zeros((1, C), F32))

    def backward(sec, n):
        v.ng[...] = jnp.zeros((M, C), F32)

        def hidden_block(b, carry):
            grad = lax.dot_general(
                v.scl[sec], v.dnw[sec, columns(b), :], CONTRACT_LAST, preferred_element_type=F32
            )
            low = (grad * v.sl[sec, b]).astype(BF16)
            scatter_pieces(v.bs, sec, b, low)
            v.bh[sec, :, columns(b)] = jnp.sum(low.astype(F32), axis=0, keepdims=True)
            v.ng[...] += lax.dot_general(
                low, v.upw[sec, :, columns(b)], CONTRACT_LAST, preferred_element_type=F32
            )
            return carry

        lax.fori_loop(0, s.NB, hidden_block, 0, unroll=True)

        def norm(i, carry):
            bias_sum, gain_sum, shift_sum = carry
            ng = v.ng[cells(i), :]
            unit = v.un[sec, cells(i), :]
            inv = v.inv[sec, cells(i), :][:, :1]
            both = ng * unit
            gained = ng * vector(sec, 1)
            mean = jnp.sum(gained, axis=-1, keepdims=True) * (1.0 / C)
            along = jnp.sum(gained * unit, axis=-1, keepdims=True) * (1.0 / C)
            grad = (inv * (gained - mean - unit * along)).astype(BF16).astype(F32)
            for j in range(STEP):
                row = grad[j * W : (j + 1) * W]
                write_row(n, i * STEP + j, row)
                for b in range(CB):
                    lanes = row[:, b * LANES : (b + 1) * LANES]
                    v.ag[0, i * STEP + j, pl.ds(b, W, stride=CB), :] = lanes
                    v.ag[1, i * STEP + j, pl.ds(CB + b, W, stride=CB), :] = lanes
            return (
                bias_sum + jnp.sum(grad, axis=0, keepdims=True),
                gain_sum + jnp.sum(both, axis=0, keepdims=True),
                shift_sum + jnp.sum(ng, axis=0, keepdims=True),
            )

        zero = jnp.zeros((1, C), F32)
        totals = lax.fori_loop(0, R // STEP, norm, (zero, zero, zero))
        for i in range(3):
            v.vs[sec, i] = totals[i]

    def through(sec, n, at, to):
        correlate(n, sec, True)

        def rows(i, carry):
            g = v.nat[at, i].astype(F32)
            v.nat[to, i] = (g + correlated(i)).astype(BF16)
            return carry

        lax.fori_loop(0, R, rows, 0)

    for copy in remote_params:
        copy.start()
    load_x.wait()

    def first_rows(i, carry):
        write_row(0, i, v.nat[0, i].astype(F32))
        return carry

    lax.fori_loop(0, R, first_rows, 0)
    for copy in halo_sends(0):
        copy.start()
    for sec in range(2):
        for i in range(7):
            wait_param(i, sec)
        for b in range(CB):
            piece = v.tp[sec, :, b * LANES : (b + 1) * LANES].astype(F32)
            v.wt[sec, pl.ds(b, taps, stride=SUB), :] = piece
            v.wt[sec, pl.ds(CB + b, taps, stride=SUB), :] = piece
    for sec in range(2):
        v.sm[sec] = jnp.zeros((SMALL_ROWS, C), F32)
    for i in range(R):
        v.ag[0, i, s.WC : s.ACC] = jnp.zeros((SUB, LANES), F32)
        v.ag[1, i, 0:SUB] = jnp.zeros((SUB, LANES), F32)
        v.ag[1, i, s.WC : s.ACC] = jnp.zeros((SUB, LANES), F32)
    load_g.wait()
    scale(1, 3)
    send_factor(3, 1)

    halo_wait(0)
    forward(0)
    for copy in halo_sends(1):
        copy.start()
    send_factor(0, 0)
    send_factor(2, 0)
    send_out(0, 0, v.nat.at[1])

    halo_wait(1)
    forward(1)
    send_factor(0, 1)
    backward(1, 2)
    for copy in halo_sends(2):
        copy.start()
    send_factor(1, 1)
    send_out(0, 1, v.nat.at[2])
    stencil(1, 1)
    branch_sum(1, 3)
    dense(1, 0)

    halo_wait(2)
    through(1, 2, 3, 4)
    scale(0, 4)
    send_factor(3, 0)
    backward(0, 3)
    for copy in halo_sends(3):
        copy.start()
    send_factor(1, 0)
    service(1, 0)
    dense(1, 1)
    dense(0, 0)
    send_out(1, 1, v.nat.at[4])
    branch_sum(0, 4)
    send_small(1)
    stencil(0, 0)
    send_small(0)
    dense(0, 1)
    halo_wait(3)
    through(0, 3, 4, 5)
    send_out(1, 0, v.nat.at[5])
    service(1, 1)
    service(0, 0)
    service(0, 1)

    total = jnp.zeros((SMALL_ROWS, s.CP), F32)
    for i in range(2 * s.PIECES):
        pltpu.make_async_copy(v.scr.at[i], v.scr.at[i], v.s_r.at[i]).wait()
        total = total + v.scr[i].astype(F32)
    for i in range(taps):
        kg_out[i] = total[i : i + 1]
    for i in range(5):
        vg_out[i] = total[taps + i : taps + i + 1]
    for j in range(bias_rows):
        row = SMALL_ROWS - SUB + j
        hb_out[:, j * s.CP : (j + 1) * s.CP] = total[row : row + 1]
    dn_out[...] = z_total(0).T
    up_out[...] = z_total(1)

    for kind in range(2):
        any_half = v.nat.at[0]

        @pl.when(c == 0)
        def _():
            out_remote(kind, 1, any_half).wait_send()
            out_local(kind, any_half).wait()

        @pl.when(c == 1)
        def _():
            out_remote(kind, 0, any_half).wait_send()
            out_local(kind, any_half).wait()

        out = so_out if kind == 0 else bg_out
        spot = out.at[:, pl.ds(pl.multiple_of((1 - c) * W, W), W), :]
        pltpu.make_async_remote_copy(
            src_ref=spot,
            dst_ref=spot,
            send_sem=v.o_s.at[kind, 1],
            recv_sem=v.o_r.at[kind],
            device_id={"segment": 1 - c},
            device_id_type=MESH,
        ).wait_recv()
    for copy in remote_params:
        copy.wait_send()
    for n in range(4):
        for copy in halo_sends(n):
            copy.wait_send()
    for sec in range(2):
        for kind in range(4):
            factor_done(kind, sec)
        small_done(sec)
    for mat in range(2):
        for i in range(L):

            @pl.when(i != l)
            def _():
                z_final(mat, i).wait_send()


def hand_out(*refs):
    count = len(refs) // 2
    for i in range(count):
        refs[count + i][...] = refs[i][...]


def local(*args):
    inputs, up_weight = args[0], args[6]
    s = sizes(inputs.shape, up_weight.shape[2])
    scratch = scratch_of(s)
    full = pl.BlockSpec(memory_space=pltpu.VMEM)
    hbm = pl.BlockSpec(memory_space=pl.ANY)
    results = (
        pl.pallas_call(
            functools.partial(body, s, tuple(scratch)),
            out_shape=[
                jax.ShapeDtypeStruct(inputs.shape, BF16),
                jax.ShapeDtypeStruct(inputs.shape, BF16),
                jax.ShapeDtypeStruct((s.C, s.CHUNK), F32),
                jax.ShapeDtypeStruct((s.CHUNK, s.C), F32),
                jax.ShapeDtypeStruct((1, s.CHUNK), F32),
                jax.ShapeDtypeStruct((KERNEL * KERNEL, 1, s.CP), F32),
                jax.ShapeDtypeStruct((5, 1, s.CP), F32),
            ],
            in_specs=[hbm] * len(args),
            out_specs=[hbm, hbm] + [full] * 5,
            scratch_shapes=list(scratch.values()),
            compiler_params=pltpu.CompilerParams(
                collective_id=0, has_side_effects=True, vmem_limit_bytes=58 * 1024 * 1024
            ),
        )(*args)
    )
    section_out, boundary_grad, up_grad, down_grad, bias_grad, kernel_grad, vector_grad = (
        pl.pallas_call(
            hand_out,
            out_shape=[jax.ShapeDtypeStruct(x.shape, x.dtype) for x in results],
            in_specs=[full] * len(results),
            out_specs=[full] * len(results),
        )(*results)
    )
    return (
        section_out[None],
        boundary_grad[None],
        up_grad[None],
        down_grad[None],
        bias_grad,
        kernel_grad.transpose(1, 0, 2),
        vector_grad.transpose(1, 0, 2),
    )


def solution(mesh):
    placed = (
        P(("groups", "lat"), "lon", None),
        P(("groups", "lat"), "lon", None),
        P("segment", None, None),
        P("segment", None),
        P("segment", None),
        P("segment", None),
        P("segment", None, None),
        P("segment", None),
        P("segment", None, None),
        P("segment", None),
        P("segment", None),
    )
    return jax.shard_map(
        local,
        mesh=mesh,
        in_specs=placed,
        out_specs=(
            P("segment", ("groups", "lat"), "lon", None),
            P("segment", ("groups", "lat"), "lon", None),
            P(("groups", "segment"), None, ("lon", "lat")),
            P(("groups", "segment"), ("lon", "lat"), None),
            P(("groups", "segment"), ("lon", "lat")),
            P(("groups", "segment"), None, ("lon", "lat")),
            P(("groups", "segment"), None, ("lon", "lat")),
        ),
        check_vma=False,
    )
```

```python
import functools
import types
import jax
import jax.numpy as jnp
from jax import lax
from jax.experimental import pallas as pl
from jax.experimental.pallas import tpu as pltpu
from jax.sharding import PartitionSpec as P

KERNEL = 7
MARGIN = KERNEL // 2
EPSILON = 1e-06
ROOT_HALF = 0.7071067811865476
DENSITY_SCALE = 0.3989422804014327
LANES = 128
SUB = 8
MESH = pl.DeviceIdType.MESH
F32 = jnp.float32
BF16 = jnp.bfloat16
CONTRACT_LAST = (((1,), (1,)), ((), ()))
SMALL_ROWS = 64
HALVES = 1


def gelu_parts(z):
    bell = jnp.exp(-0.5 * z * z)
    d = 1.0 + (0.3275911 * ROOT_HALF) * jnp.abs(z)
    r = pl.reciprocal(d, approx=True)
    r = r * (2.0 - d * r)
    poly = r * (
        0.127414796
        + r * (-0.142248368 + r * (0.7107068705 + r * (-0.7265760135 + r * 0.5307027145)))
    )
    tail = poly * bell
    cumulative = jnp.where(z >= 0.0, 1.0 - tail, tail)
    return z * cumulative, cumulative + z * (bell * DENSITY_SCALE)


def sizes(inputs_shape, hidden):
    s = types.SimpleNamespace()
    s.L, s.T = lax.axis_size("lon"), lax.axis_size("lat")
    s.R, s.W, s.C = inputs_shape[0], inputs_shape[1] // 2, inputs_shape[2]
    s.M = s.R * s.W
    s.HID = hidden
    s.CB = s.C // LANES
    assert s.CB * 2 == SUB
    s.I0 = 4 * s.CB
    s.WC = s.W * s.CB
    s.COLS = s.WC + 2 * s.I0
    s.ACC = s.WC + SUB
    s.PIECES = s.L * s.T
    s.CHUNK = hidden // s.PIECES
    s.CP = s.C // s.PIECES
    s.BN = max(s.CHUNK, 256)
    s.NB = hidden // s.BN
    s.K = 2 * s.T * s.M
    s.NP = 2 * s.L
    return s


def scratch_of(s):
    dma = pltpu.SemaphoreType.DMA
    vm = pltpu.VMEM
    return dict(
        nat=vm((6, s.R, s.W, s.C), BF16),
        p0=vm((4, s.R + 2 * MARGIN, s.COLS, LANES), F32),
        pb=vm((4, s.R + 2 * MARGIN, s.COLS, LANES), BF16),
        wt=vm((2, KERNEL * KERNEL * SUB, LANES), F32),
        a=vm((2, s.R, s.ACC, LANES), F32),
        ag=vm((2, s.R, s.ACC, LANES), F32),
        kg=vm((KERNEL * KERNEL * SUB, LANES), F32),
        tp=vm((2, KERNEL * KERNEL, s.C), BF16),
        vec=vm((2, 5, 1, s.C), F32),
        hbi=vm((2, 1, s.HID), F32),
        upw=vm((2, s.C, s.HID), BF16),
        dnw=vm((2, s.HID, s.C), BF16),
        un=vm((2, s.M, s.C), F32),
        inv=vm((2, s.M, LANES), F32),
        br=vm((2, s.M, s.C), F32),
        ng=vm((s.M, s.C), F32),
        sl=vm((2, s.NB, s.M, s.BN), F32),
        nrm=vm((s.M, s.C), BF16),
        scl=vm((2, s.M, s.C), BF16),
        hs=vm((2, s.T, s.L, s.M, s.CHUNK), BF16),
        bs=vm((2, s.T, s.L, s.M, s.CHUNK), BF16),
        nts=vm((2, s.C, s.M), BF16),
        sts=vm((2, s.C, s.M), BF16),
        hr=vm((s.L, s.K, s.CHUNK), BF16),
        bgr=vm((s.L, s.K, s.CHUNK), BF16),
        nr=vm((2 * s.T, s.C, s.M), BF16),
        sr=vm((2 * s.T, s.C, s.M), BF16),
        zs=vm((2, s.L, s.C, s.CHUNK), BF16),
        zm=vm((2, s.L, s.C, s.CHUNK), BF16),
        zr=vm((2, s.L // 2, s.C, s.CHUNK), BF16),
        zo=vm((2, s.C, s.CHUNK), F32),
        vs=vm((2, 5, 1, s.C), F32),
        sm=vm((2, SMALL_ROWS, s.C), F32),
        bh=vm((2, 1, s.HID), F32),
        sc=vm((2, s.PIECES, SMALL_ROWS // 2, 2 * s.CP), BF16),
        sib=vm((s.PIECES, SMALL_ROWS // 2, 2 * s.CP), BF16),
        scr=vm((s.PIECES, SMALL_ROWS // 2, 2 * s.CP), BF16),
        load=dma((4,)),
        prm_l=dma((7 + 2 * HALVES,)),
        prm_s=dma((7 + 2 * HALVES,)),
        prm_r=dma((7 + 2 * HALVES,)),
        halo_s=dma((4, 8)),
        halo_r=dma((4, 8)),
        f_s=dma((2, 4, s.T, s.L)),
        f_r=dma((4, 2 * s.T, s.L)),
        z_s=dma((2, s.L)),
        zm_r=dma((2, s.L)),
        z_r=dma((2, s.L // 2)),
        s_s=dma((s.PIECES,)),
        s_r=dma((s.PIECES,)),
        o_s=dma((2, 2)),
        o_r=dma((2,)),
    )


def body(s, names, *refs):
    (x_in, g_in, k_in, cb_in, gain_in, shift_in, up_in, hb_in, dn_in, ob_in, ls_in) = refs[:11]
    so_out, bg_out, up_out, dn_out, hb_out, kg_out, vg_out = refs[11:18]
    v = types.SimpleNamespace(**dict(zip(names, refs[18:])))
    R, W, C, M, L, T, NP, CB = s.R, s.W, s.C, s.M, s.L, s.T, s.NP, s.CB
    c = lax.axis_index("segment")
    l = lax.axis_index("lon")
    t = lax.axis_index("lat")
    p = 2 * l + c
    north = t == 0
    south = t == T - 1

    def cell_at(place, row):
        return {"lat": row, "lon": place // 2, "segment": place % 2}

    def turn(place):
        return (place + NP) % NP

    own_cols = pl.ds(pl.multiple_of(c * W, W), W)
    load_x = pltpu.make_async_copy(x_in.at[:, own_cols, :], v.nat.at[0], v.load.at[0])
    load_g = pltpu.make_async_copy(g_in.at[:, own_cols, :], v.nat.at[3], v.load.at[1])
    load_x.start()
    load_g.start()
    params = [
        (k_in.at[0], v.tp.at[c]),
        (cb_in, v.vec.at[c, 0]),
        (gain_in, v.vec.at[c, 1]),
        (shift_in, v.vec.at[c, 2]),
        (ob_in, v.vec.at[c, 3]),
        (ls_in, v.vec.at[c, 4]),
        (hb_in, v.hbi.at[c]),
    ]
    width = s.HID // HALVES
    for h in range(HALVES):
        cols = pl.ds(h * width, width)
        params.append((up_in.at[0, :, cols], v.upw.at[c, :, cols]))
        params.append((dn_in.at[0, cols, :], v.dnw.at[c, cols, :]))
    local_params = [
        pltpu.make_async_copy(src, dst, v.prm_l.at[i]) for i, (src, dst) in enumerate(params)
    ]
    remote_params = [
        pltpu.make_async_remote_copy(
            src_ref=src,
            dst_ref=dst,
            send_sem=v.prm_s.at[i],
            recv_sem=v.prm_r.at[i],
            device_id={"segment": 1 - c},
            device_id_type=MESH,
        )
        for i, (src, dst) in enumerate(params)
    ]
    for copy in local_params:
        copy.start()

    barrier = pltpu.get_barrier_semaphore()
    for dl in range(L):
        for dt in range(T):
            for dc in range(2):
                if dl or dt or dc:
                    pl.semaphore_signal(
                        barrier,
                        inc=1,
                        device_id={
                            "lat": lax.rem(t + dt, T),
                            "lon": lax.rem(l + dl, L),
                            "segment": lax.rem(c + dc, 2),
                        },
                        device_id_type=MESH,
                    )

    mid = pl.ds(s.I0, s.WC)
    first_cols, last_cols = pl.ds(s.I0, s.I0), pl.ds(s.WC, s.I0)
    left_pad, right_pad = pl.ds(0, s.I0), pl.ds(s.I0 + s.WC, s.I0)
    top_rows, low_rows, own_rows = pl.ds(0, MARGIN), pl.ds(R + MARGIN, MARGIN), pl.ds(MARGIN, R)
    regions = [
        (top_rows, mid),
        (top_rows, left_pad),
        (top_rows, right_pad),
        (low_rows, mid),
        (low_rows, left_pad),
        (low_rows, right_pad),
        (own_rows, left_pad),
        (own_rows, right_pad),
    ]
    half = NP // 2
    up_t, up_p = jnp.where(north, t, t - 1), jnp.where(north, p + half, p)
    dn_t, dn_p = jnp.where(south, t, t + 1), jnp.where(south, p + half, p)
    up_to, up_region = jnp.where(north, 0, R + MARGIN), jnp.where(north, 0, 3)
    dn_to, dn_region = jnp.where(south, R + MARGIN, 0), jnp.where(south, 3, 0)

    def halo_sends(n):
        head, tail = pl.ds(MARGIN, MARGIN), pl.ds(R, MARGIN)
        up_rows, dn_rows = pl.ds(up_to, MARGIN), pl.ds(dn_to, MARGIN)
        plans = [
            (own_rows, first_cols, own_rows, right_pad, 7, p - 1, t),
            (own_rows, last_cols, own_rows, left_pad, 6, p + 1, t),
            (head, mid, up_rows, mid, up_region, up_p, up_t),
            (tail, mid, dn_rows, mid, dn_region, dn_p, dn_t),
            (head, first_cols, up_rows, right_pad, up_region + 2, up_p - 1, up_t),
            (head, last_cols, up_rows, left_pad, up_region + 1, up_p + 1, up_t),
            (tail, first_cols, dn_rows, right_pad, dn_region + 2, dn_p - 1, dn_t),
            (tail, last_cols, dn_rows, left_pad, dn_region + 1, dn_p + 1, dn_t),
        ]
        return [
            pltpu.make_async_remote_copy(
                src_ref=v.pb.at[n, rows, cols],
                dst_ref=v.pb.at[n, to_rows, to_cols],
                send_sem=v.halo_s.at[n, i],
                recv_sem=v.halo_r.at[n, region],
                device_id=cell_at(turn(place), row),
                device_id_type=MESH,
            )
            for i, (rows, cols, to_rows, to_cols, region, place, row) in enumerate(plans)
        ]

    def region_wait(n, g):
        rows, cols = regions[g]
        spot = v.pb.at[n, rows, cols]
        pltpu.make_async_copy(spot, spot, v.halo_r.at[n, g]).wait()

    def wait_sides(n):
        region_wait(n, 6)
        region_wait(n, 7)

        def sides(i, carry):
            v.p0[n, i, left_pad] = v.pb[n, i, left_pad].astype(F32)
            v.p0[n, i, right_pad] = v.pb[n, i, right_pad].astype(F32)
            return carry

        lax.fori_loop(MARGIN, R + MARGIN, sides, 0)

    def wait_rows(n):
        for g in range(6):
            region_wait(n, g)
        for a in range(MARGIN):
            up_at = jnp.where(north, MARGIN - 1 - a, a)
            dn_at = R + MARGIN + jnp.where(south, MARGIN - 1 - a, a)
            v.p0[n, up_at] = v.pb[n, a].astype(F32)
            v.p0[n, dn_at] = v.pb[n, R + MARGIN + a].astype(F32)

    def write_row(n, i, value):
        row = i + MARGIN
        for b in range(CB):
            v.p0[n, row, pl.ds(s.I0 + b, W, stride=CB), :] = value[:, b * LANES : (b + 1) * LANES]
        v.pb[n, row, mid] = v.p0[n, row, mid].astype(BF16)

    def correlate(n, sec, backward):
        def weight(index):
            return v.wt[sec, pl.ds(pl.multiple_of(index * SUB, SUB), SUB), :]

        def tap(r, q):
            return (KERNEL * KERNEL - 1 if backward else 0) + (-1 if backward else 1) * (
                KERNEL * r + q
            )

        def edge_tap(r, q, pole):
            if backward:
                return jnp.where(pole, KERNEL * r + KERNEL - 1 - q, tap(r, q))
            return tap(r, q)

        def at_of(k, q):
            return pl.ds(pl.multiple_of(SUB * k + SUB * ((q + 1) // 2), SUB), SUB)

        wait_sides(n)
        for parity in range(2):
            col_taps = range(1 - parity, KERNEL, 2)

            def step(k, carry):
                total = jnp.zeros((R, SUB, LANES), F32)
                for q in col_taps:
                    rows = v.p0[n, own_rows, at_of(k, q), :]
                    for r in range(KERNEL):
                        low, high = max(0, MARGIN - r), min(R, R + MARGIN - r)
                        term = rows[low + r - MARGIN : high + r - MARGIN] * weight(tap(r, q))
                        middle = total[low:high] + term
                        if high < R:
                            total = jnp.concatenate([middle, total[high:]], axis=0)
                        elif low > 0:
                            total = jnp.concatenate([total[:low], middle], axis=0)
                        else:
                            total = middle
                v.a[parity, :, pl.ds(pl.multiple_of(SUB * k, SUB), SUB), :] = total
                return carry

            lax.fori_loop(0, s.WC // SUB + parity, step, 0)

        wait_rows(n)
        for parity in range(2):
            col_taps = range(1 - parity, KERNEL, 2)

            def step(k, carry):
                spot = pl.ds(pl.multiple_of(SUB * k, SUB), SUB)
                upper = v.a[parity, 0:MARGIN, spot, :]
                lower = v.a[parity, R - MARGIN : R, spot, :]
                for q in col_taps:
                    above = v.p0[n, top_rows, at_of(k, q), :]
                    below = v.p0[n, low_rows, at_of(k, q), :]
                    for r in range(MARGIN):
                        cut = MARGIN - r
                        part = upper[:cut] + above[r:] * weight(edge_tap(r, q, north))
                        upper = jnp.concatenate([part, upper[cut:]], axis=0) if r else part
                        far = KERNEL - 1 - r
                        part = lower[r:] + below[:cut] * weight(edge_tap(far, q, south))
                        lower = jnp.concatenate([lower[:r], part], axis=0) if r else part
                v.a[parity, 0:MARGIN, spot, :] = upper
                v.a[parity, R - MARGIN : R, spot, :] = lower
                return carry

            lax.fori_loop(0, s.WC // SUB + parity, step, 0)

    def correlated(i):
        return jnp.concatenate(
            [
                v.a[0, i, pl.ds(b, W, stride=CB), :] + v.a[1, i, pl.ds(CB + b, W, stride=CB), :]
                for b in range(CB)
            ],
            axis=1,
        )

    def stencil(n, sec):
        for q in range(KERNEL):
            parity = 1 - q % 2

            def step(k, totals):
                grad = v.ag[parity, :, pl.ds(pl.multiple_of(SUB * k, SUB), SUB), :]
                at = pl.multiple_of(SUB * k + SUB * ((q + 1) // 2), SUB)
                rows = v.p0[n, :, pl.ds(at, SUB), :]
                return tuple(
                    totals[r] + jnp.sum(rows[r : r + R] * grad, axis=0) for r in range(KERNEL)
                )

            zero = jnp.zeros((SUB, LANES), F32)
            totals = lax.fori_loop(0, s.WC // SUB + parity, step, (zero,) * KERNEL)
            for r in range(KERNEL):
                v.kg[pl.ds((KERNEL * r + q) * SUB, SUB), :] = totals[r]
        count = KERNEL * KERNEL
        for b in range(CB):
            v.sm[sec, 0:count, b * LANES : (b + 1) * LANES] = (
                v.kg[pl.ds(b, count, stride=SUB), :] + v.kg[pl.ds(CB + b, count, stride=SUB), :]
            )

    source = t * 2 + c
    place_k = pl.ds(pl.multiple_of(source * M, M), M)
    even = lax.rem(l, 2) == 0
    partner = l + 1 - 2 * lax.rem(l, 2)

    def z_to(i):
        to = jnp.where(even, L - 1 - i, i)
        beyond = jnp.where(even, to > l, to < l)
        return to, beyond

    def factor(kind, sec, dt, to):
        row = lax.rem(t + dt, T)
        if kind == 0:
            return v.hs.at[sec, row, to], v.hr.at[to, place_k, :]
        if kind == 1:
            return v.bs.at[sec, row, to], v.bgr.at[to, place_k, :]
        if kind == 2:
            return v.nts.at[sec], v.nr.at[source]
        return v.sts.at[sec], v.sr.at[source]

    def factor_remote(kind, sec, dt, to):
        src, dst = factor(kind, sec, dt, to)
        return pltpu.make_async_remote_copy(
            src_ref=src,
            dst_ref=dst,
            send_sem=v.f_s.at[sec, kind, dt, to],
            recv_sem=v.f_r.at[kind, source, to],
            device_id={"lat": lax.rem(t + dt, T), "segment": sec},
            device_id_type=MESH,
        )

    def factor_local(kind, sec, to):
        src, dst = factor(kind, sec, 0, to)
        return pltpu.make_async_copy(src, dst, v.f_r.at[kind, source, to])

    def send_factor(kind, sec):
        for i in range(L if kind < 2 else 1):
            to = z_to(i)[0] if kind < 2 else 0
            for dt in range(1, T):
                factor_remote(kind, sec, dt, to).start()

            @pl.when(c == sec)
            def _():
                factor_local(kind, sec, to).start()

            @pl.when(c != sec)
            def _():
                factor_remote(kind, sec, 0, to).start()

    def factor_done(kind, sec):
        for to in range(L if kind < 2 else 1):
            for dt in range(1, T):
                factor_remote(kind, sec, dt, to).wait_send()

            @pl.when(c != sec)
            def _():
                factor_remote(kind, sec, 0, to).wait_send()

    def factor_wait(kind, to):
        for d in range(2 * T):
            rows = pl.ds(d * M, M)
            if kind == 0:
                spot = v.hr.at[to, rows, :]
            elif kind == 1:
                spot = v.bgr.at[to, rows, :]
            else:
                spot = (v.nr if kind == 2 else v.sr).at[d]
            pltpu.make_async_copy(spot, spot, v.f_r.at[kind, d, to]).wait()

    def z_merge(mat, to):
        return pltpu.make_async_remote_copy(
            src_ref=v.zs.at[mat, to],
            dst_ref=v.zm.at[mat, to],
            send_sem=v.z_s.at[mat, to],
            recv_sem=v.zm_r.at[mat, to],
            device_id={"lon": partner},
            device_id_type=MESH,
        )

    def z_final(mat, to):
        return pltpu.make_async_remote_copy(
            src_ref=v.zs.at[mat, to],
            dst_ref=v.zr.at[mat, l // 2],
            send_sem=v.z_s.at[mat, to],
            recv_sem=v.z_r.at[mat, l // 2],
            device_id={"lon": to},
            device_id_type=MESH,
        )

    def dense(sec, mat):
        @pl.when(c == sec)
        def _():
            left, right = (v.sr, v.hr) if mat == 0 else (v.nr, v.bgr)
            factor_wait(3 if mat == 0 else 2, 0)
            for i in range(L):
                to, beyond = z_to(i)
                factor_wait(0 if mat == 0 else 1, to)
                wide = jnp.concatenate([left[d] for d in range(2 * T)], axis=1)
                term = jnp.dot(wide, right[to], preferred_element_type=F32)

                @pl.when(beyond)
                def _():
                    v.zs[mat, to] = term.astype(BF16)

                    @pl.when(to == partner)
                    def _():
                        z_final(mat, to).start()

                    @pl.when(to != partner)
                    def _():
                        z_merge(mat, to).start()

                @pl.when(to == l)
                def _():
                    v.zo[mat] = term

                @pl.when(jnp.logical_not(jnp.logical_or(beyond, to == l)))
                def _():
                    v.zs[mat, to] = term.astype(BF16)

    def service(sec, mat):
        @pl.when(c == sec)
        def _():
            for i in range(L):
                to, beyond = z_to(i)

                @pl.when(jnp.logical_and(jnp.logical_not(beyond), to != l))
                def _():
                    z_merge(mat, to).wait_recv()
                    total = v.zs[mat, to].astype(F32) + v.zm[mat, to].astype(F32)
                    v.zs[mat, to] = total.astype(BF16)
                    z_final(mat, to).start()

    def z_total(mat):
        total = v.zo[mat]
        for j in range(L // 2):
            spot = v.zr.at[mat, j]
            pltpu.make_async_copy(spot, spot, v.z_r.at[mat, j]).wait()
            total = total + v.zr[mat, j].astype(F32)
        return total

    def small_sibling(sec):
        return pltpu.make_async_remote_copy(
            src_ref=v.sc.at[sec],
            dst_ref=v.sib,
            send_sem=v.s_s.at[0],
            recv_sem=v.s_r.at[0],
            device_id={"segment": sec},
            device_id_type=MESH,
        )

    def small_remote(sec, dl, dt):
        to_l, to_t = lax.rem(l + dl, L), lax.rem(t + dt, T)
        return pltpu.make_async_remote_copy(
            src_ref=v.sc.at[sec, to_l * T + to_t],
            dst_ref=v.scr.at[dl * T + dt],
            send_sem=v.s_s.at[dl * T + dt],
            recv_sem=v.s_r.at[dl * T + dt],
            device_id={"lat": to_t, "lon": to_l},
            device_id_type=MESH,
        )

    taps = KERNEL * KERNEL
    bias_rows = s.HID // C
    away = [(dl, dt) for dl in range(L) for dt in range(T) if dl or dt]

    def send_small(sec):
        half_rows = SMALL_ROWS // 2
        for i in range(5):
            v.sm[sec, taps + i : taps + i + 1, :] = v.vs[sec, i]
        for piece in range(s.PIECES):
            rows = jnp.concatenate(
                [
                    v.bh[sec, :, piece * s.CHUNK + j * s.CP : piece * s.CHUNK + (j + 1) * s.CP]
                    for j in range(bias_rows)
                ]
                + [jnp.zeros((SUB - bias_rows, s.CP), F32)],
                axis=0,
            )
            block = v.sm[sec, :, piece * s.CP : (piece + 1) * s.CP]
            low = jnp.concatenate(
                [block[half_rows : SMALL_ROWS - SUB], block[SMALL_ROWS - SUB :] + rows], axis=0
            )
            v.sc[sec, piece] = jnp.concatenate([block[:half_rows], low], axis=1).astype(BF16)

        @pl.when(c != sec)
        def _():
            small_sibling(sec).start()

    def merge_small(sec):
        @pl.when(c == sec)
        def _():
            pltpu.make_async_copy(v.sib, v.sib, v.s_r.at[0]).wait()
            for piece in range(s.PIECES):
                total = v.sc[sec, piece].astype(F32) + v.sib[piece].astype(F32)
                v.sc[sec, piece] = total.astype(BF16)
            for dl, dt in away:
                small_remote(sec, dl, dt).start()

    def out_remote(kind, sec, source):
        out = so_out if kind == 0 else bg_out
        return pltpu.make_async_remote_copy(
            src_ref=source,
            dst_ref=out.at[:, own_cols, :],
            send_sem=v.o_s.at[kind, 1],
            recv_sem=v.o_r.at[kind],
            device_id={"segment": sec},
            device_id_type=MESH,
        )

    def out_local(kind, source):
        out = so_out if kind == 0 else bg_out
        return pltpu.make_async_copy(source, out.at[:, own_cols, :], v.o_s.at[kind, 0])

    def send_out(kind, sec, source):
        @pl.when(c == sec)
        def _():
            out_local(kind, source).start()

        @pl.when(c != sec)
        def _():
            out_remote(kind, sec, source).start()

    def vector(sec, which):
        return v.vec[sec, which]

    def wait_param(i, sec):
        @pl.when(c == sec)
        def _():
            local_params[i].wait()

        @pl.when(c != sec)
        def _():
            src, _ = params[i]
            spot = [v.tp.at[sec]] + [v.vec.at[sec, j] for j in range(5)]
            spot = spot + [v.hbi.at[sec]]
            for h in range(HALVES):
                cols = pl.ds(h * width, width)
                spot = spot + [v.upw.at[sec, :, cols], v.dnw.at[sec, cols, :]]
            spot = spot[i]
            pltpu.make_async_remote_copy(
                src_ref=spot,
                dst_ref=spot,
                send_sem=v.prm_s.at[i],
                recv_sem=v.prm_r.at[i],
                device_id={"segment": 1 - c},
                device_id_type=MESH,
            ).wait_recv()

    STEP = 2
    CELLS = STEP * W

    def block(ref, i):
        return jnp.concatenate([ref[i * STEP + j] for j in range(STEP)], axis=0)

    def cells(i):
        return pl.ds(pl.multiple_of(i * CELLS, CELLS), CELLS)

    def transpose_into(target, source):
        for b in range(CB):
            piece = source[:, b * LANES : (b + 1) * LANES].astype(F32)
            target[b * LANES : (b + 1) * LANES, :] = piece.T.astype(BF16)

    per = s.BN // s.CHUNK

    def scatter_pieces(ref, sec, b, value):
        for j in range(per):
            index = b * per + j
            ref[sec, lax.rem(index, T), index // T] = value[:, j * s.CHUNK : (j + 1) * s.CHUNK]

    def columns(b):
        return pl.ds(pl.multiple_of(b * s.BN, s.BN), s.BN)

    def forward(sec):
        correlate(sec, sec, False)

        def norm(i, carry):
            x = jnp.concatenate([correlated(i * STEP + j) for j in range(STEP)], axis=0)
            x = x + vector(sec, 0)
            mean = jnp.sum(x, axis=-1, keepdims=True) * (1.0 / C)
            x = x - mean
            var = jnp.sum(x * x, axis=-1, keepdims=True) * (1.0 / C)
            inv = lax.rsqrt(var + EPSILON)
            unit = x * inv
            v.un[sec, cells(i), :] = unit
            v.inv[sec, cells(i), :] = jnp.broadcast_to(inv, (CELLS, LANES))
            v.nrm[cells(i), :] = (unit * vector(sec, 1) + vector(sec, 2)).astype(BF16)
            return carry

        lax.fori_loop(0, R // STEP, norm, 0)
        transpose_into(v.nts.at[sec], v.nrm)
        if sec == 1:
            send_factor(2, 1)
        v.br[sec] = jnp.broadcast_to(vector(sec, 3), (M, C))

        def hidden_block(b, carry):
            before = (
                jnp.dot(v.nrm[...], v.upw[sec, :, columns(b)], preferred_element_type=F32)
                + v.hbi[sec, :, columns(b)]
            )
            active, slope = gelu_parts(before)
            v.sl[sec, b] = slope
            active = active.astype(BF16)
            scatter_pieces(v.hs, sec, b, active)
            v.br[sec] += jnp.dot(active, v.dnw[sec, columns(b), :], preferred_element_type=F32)
            return carry

        step = s.NB // HALVES
        for h in range(HALVES):
            wait_param(7 + 2 * h, sec)
            wait_param(8 + 2 * h, sec)
            lax.fori_loop(h * step, (h + 1) * step, hidden_block, 0, unroll=True)

        def finish(i, carry):
            u = block(v.nat.at[sec], i).astype(F32)
            u = (u + vector(sec, 4) * v.br[sec, cells(i), :]).astype(BF16)
            for j in range(STEP):
                row = u[j * W : (j + 1) * W]
                v.nat[sec + 1, i * STEP + j] = row
                if sec == 0:
                    write_row(1, i * STEP + j, row.astype(F32))
            return carry

        lax.fori_loop(0, R // STEP, finish, 0)

    def scale(sec, at):
        def rows(i, carry):
            g = block(v.nat.at[at], i).astype(F32)
            low = (g * vector(sec, 4)).astype(BF16)
            v.scl[sec, cells(i), :] = low
            return carry + jnp.sum(low.astype(F32), axis=0, keepdims=True)

        v.vs[sec, 3] = lax.fori_loop(0, R // STEP, rows, jnp.zeros((1, C), F32))
        transpose_into(v.sts.at[sec], v.scl.at[sec])

    def branch_sum(sec, at):
        def rows(i, carry):
            g = block(v.nat.at[at], i).astype(F32)
            return carry + jnp.sum(g * v.br[sec, cells(i), :], axis=0, keepdims=True)

        v.vs[sec, 4] = lax.fori_loop(0, R // STEP, rows, jnp.zeros((1, C), F32))

    def backward(sec, n):
        v.ng[...] = jnp.zeros((M, C), F32)

        def hidden_block(b, carry):
            grad = lax.dot_general(
                v.scl[sec], v.dnw[sec, columns(b), :], CONTRACT_LAST, preferred_element_type=F32
            )
            low = (grad * v.sl[sec, b]).astype(BF16)
            scatter_pieces(v.bs, sec, b, low)
            v.bh[sec, :, columns(b)] = jnp.sum(low.astype(F32), axis=0, keepdims=True)
            v.ng[...] += lax.dot_general(
                low, v.upw[sec, :, columns(b)], CONTRACT_LAST, preferred_element_type=F32
            )
            return carry

        lax.fori_loop(0, s.NB, hidden_block, 0, unroll=True)

        def norm(i, carry):
            bias_sum, gain_sum, shift_sum = carry
            ng = v.ng[cells(i), :]
            unit = v.un[sec, cells(i), :]
            inv = v.inv[sec, cells(i), :][:, :1]
            both = ng * unit
            gained = ng * vector(sec, 1)
            mean = jnp.sum(gained, axis=-1, keepdims=True) * (1.0 / C)
            along = jnp.sum(gained * unit, axis=-1, keepdims=True) * (1.0 / C)
            grad = (inv * (gained - mean - unit * along)).astype(BF16).astype(F32)
            for j in range(STEP):
                row = grad[j * W : (j + 1) * W]
                write_row(n, i * STEP + j, row)
                for b in range(CB):
                    lanes = row[:, b * LANES : (b + 1) * LANES]
                    v.ag[0, i * STEP + j, pl.ds(b, W, stride=CB), :] = lanes
                    v.ag[1, i * STEP + j, pl.ds(CB + b, W, stride=CB), :] = lanes
            return (
                bias_sum + jnp.sum(grad, axis=0, keepdims=True),
                gain_sum + jnp.sum(both, axis=0, keepdims=True),
                shift_sum + jnp.sum(ng, axis=0, keepdims=True),
            )

        zero = jnp.zeros((1, C), F32)
        totals = lax.fori_loop(0, R // STEP, norm, (zero, zero, zero))
        for i in range(3):
            v.vs[sec, i] = totals[i]

    def through(sec, n, at, to):
        correlate(n, sec, True)

        def rows(i, carry):
            g = v.nat[at, i].astype(F32)
            v.nat[to, i] = (g + correlated(i)).astype(BF16)
            return carry

        lax.fori_loop(0, R, rows, 0)

    load_x.wait()

    def first_rows(i, carry):
        write_row(0, i, v.nat[0, i].astype(F32))
        return carry

    lax.fori_loop(0, R, first_rows, 0)
    for sec in range(2):
        v.sm[sec] = jnp.zeros((SMALL_ROWS, C), F32)
    for i in range(R):
        v.ag[0, i, s.WC : s.ACC] = jnp.zeros((SUB, LANES), F32)
        v.ag[1, i, 0:SUB] = jnp.zeros((SUB, LANES), F32)
        v.ag[1, i, s.WC : s.ACC] = jnp.zeros((SUB, LANES), F32)
    pl.semaphore_wait(barrier, 2 * L * T - 1)
    for copy in halo_sends(0) + remote_params:
        copy.start()
    for sec in range(2):
        for i in range(7):
            wait_param(i, sec)
        for b in range(CB):
            piece = v.tp[sec, :, b * LANES : (b + 1) * LANES].astype(F32)
            v.wt[sec, pl.ds(b, taps, stride=SUB), :] = piece
            v.wt[sec, pl.ds(CB + b, taps, stride=SUB), :] = piece
    load_g.wait()
    scale(1, 3)
    send_factor(3, 1)

    forward(0)
    for copy in halo_sends(1):
        copy.start()
    send_factor(0, 0)
    send_out(0, 0, v.nat.at[1])

    forward(1)
    send_factor(0, 1)
    backward(1, 2)
    for copy in halo_sends(2):
        copy.start()
    send_factor(1, 1)
    send_out(0, 1, v.nat.at[2])
    stencil(1, 1)
    branch_sum(1, 3)
    dense(1, 0)

    through(1, 2, 3, 4)
    scale(0, 4)
    send_factor(3, 0)
    send_factor(2, 0)
    backward(0, 3)
    for copy in halo_sends(3):
        copy.start()
    send_factor(1, 0)
    service(1, 0)
    dense(1, 1)
    dense(0, 0)
    send_out(1, 1, v.nat.at[4])
    branch_sum(0, 4)
    send_small(1)
    stencil(0, 0)
    send_small(0)
    merge_small(1)
    service(1, 1)
    merge_small(0)
    dense(0, 1)
    service(0, 0)
    through(0, 3, 4, 5)
    send_out(1, 0, v.nat.at[5])
    service(0, 1)

    sums = v.sc[c, l * T + t].astype(F32)
    for dl, dt in away:
        spot = v.scr.at[dl * T + dt]
        pltpu.make_async_copy(spot, spot, v.s_r.at[dl * T + dt]).wait()
        sums = sums + v.scr[dl * T + dt].astype(F32)
    total = jnp.concatenate([sums[:, : s.CP], sums[:, s.CP :]], axis=0)
    for i in range(taps):
        kg_out[i] = total[i : i + 1]
    for i in range(5):
        vg_out[i] = total[taps + i : taps + i + 1]
    for j in range(bias_rows):
        row = SMALL_ROWS - SUB + j
        hb_out[:, j * s.CP : (j + 1) * s.CP] = total[row : row + 1]
    dn_out[...] = z_total(0).T
    up_out[...] = z_total(1)

    for kind in range(2):
        any_half = v.nat.at[0]

        @pl.when(c == 0)
        def _():
            out_remote(kind, 1, any_half).wait_send()
            out_local(kind, any_half).wait()

        @pl.when(c == 1)
        def _():
            out_remote(kind, 0, any_half).wait_send()
            out_local(kind, any_half).wait()

        out = so_out if kind == 0 else bg_out
        spot = out.at[:, pl.ds(pl.multiple_of((1 - c) * W, W), W), :]
        pltpu.make_async_remote_copy(
            src_ref=spot,
            dst_ref=spot,
            send_sem=v.o_s.at[kind, 1],
            recv_sem=v.o_r.at[kind],
            device_id={"segment": 1 - c},
            device_id_type=MESH,
        ).wait_recv()
    for copy in remote_params:
        copy.wait_send()
    for n in range(4):
        for copy in halo_sends(n):
            copy.wait_send()
    for sec in range(2):
        for kind in range(4):
            factor_done(kind, sec)
    small_sibling(1 - c).wait_send()
    for dl, dt in away:
        small_remote(c, dl, dt).wait_send()
    for mat in range(2):
        for i in range(L):

            @pl.when(i != l)
            def _():
                z_final(mat, i).wait_send()


def hand_out(*refs):
    count = len(refs) // 2
    for i in range(count):
        refs[count + i][...] = refs[i][...]


def local(*args):
    inputs, up_weight = args[0], args[6]
    s = sizes(inputs.shape, up_weight.shape[2])
    scratch = scratch_of(s)
    full = pl.BlockSpec(memory_space=pltpu.VMEM)
    hbm = pl.BlockSpec(memory_space=pl.ANY)
    results = (
        pl.pallas_call(
            functools.partial(body, s, tuple(scratch)),
            out_shape=[
                jax.ShapeDtypeStruct(inputs.shape, BF16),
                jax.ShapeDtypeStruct(inputs.shape, BF16),
                jax.ShapeDtypeStruct((s.C, s.CHUNK), F32),
                jax.ShapeDtypeStruct((s.CHUNK, s.C), F32),
                jax.ShapeDtypeStruct((1, s.CHUNK), F32),
                jax.ShapeDtypeStruct((KERNEL * KERNEL, 1, s.CP), F32),
                jax.ShapeDtypeStruct((5, 1, s.CP), F32),
            ],
            in_specs=[hbm] * len(args),
            out_specs=[hbm, hbm] + [full] * 5,
            scratch_shapes=list(scratch.values()),
            compiler_params=pltpu.CompilerParams(
                collective_id=0, has_side_effects=True, vmem_limit_bytes=58 * 1024 * 1024
            ),
        )(*args)
    )
    section_out, boundary_grad, up_grad, down_grad, bias_grad, kernel_grad, vector_grad = (
        pl.pallas_call(
            hand_out,
            out_shape=[jax.ShapeDtypeStruct(x.shape, x.dtype) for x in results],
            in_specs=[full] * len(results),
            out_specs=[full] * len(results),
        )(*results)
    )
    return (
        section_out[None],
        boundary_grad[None],
        up_grad[None],
        down_grad[None],
        bias_grad,
        kernel_grad.transpose(1, 0, 2),
        vector_grad.transpose(1, 0, 2),
    )


def solution(mesh):
    placed = (
        P(("groups", "lat"), "lon", None),
        P(("groups", "lat"), "lon", None),
        P("segment", None, None),
        P("segment", None),
        P("segment", None),
        P("segment", None),
        P("segment", None, None),
        P("segment", None),
        P("segment", None, None),
        P("segment", None),
        P("segment", None),
    )
    return jax.shard_map(
        local,
        mesh=mesh,
        in_specs=placed,
        out_specs=(
            P("segment", ("groups", "lat"), "lon", None),
            P("segment", ("groups", "lat"), "lon", None),
            P(("groups", "segment"), None, ("lon", "lat")),
            P(("groups", "segment"), ("lon", "lat"), None),
            P(("groups", "segment"), ("lon", "lat")),
            P(("groups", "segment"), None, ("lon", "lat")),
            P(("groups", "segment"), None, ("lon", "lat")),
        ),
        check_vma=False,
    )
```

```python
import functools
import types
import jax
import jax.numpy as jnp
from jax import lax
from jax.experimental import pallas as pl
from jax.experimental.pallas import tpu as pltpu
from jax.sharding import PartitionSpec as P

KERNEL = 7
MARGIN = KERNEL // 2
EPSILON = 1e-06
ROOT_HALF = 0.7071067811865476
DENSITY_SCALE = 0.3989422804014327
LANES = 128
SUB = 8
MESH = pl.DeviceIdType.MESH
F32 = jnp.float32
BF16 = jnp.bfloat16
CONTRACT_LAST = (((1,), (1,)), ((), ()))
SMALL_ROWS = 64
HALVES = 1


def gelu_parts(z):
    bell = jnp.exp(-0.5 * z * z)
    d = 1.0 + (0.3275911 * ROOT_HALF) * jnp.abs(z)
    r = pl.reciprocal(d, approx=True)
    r = r * (2.0 - d * r)
    poly = r * (
        0.127414796
        + r * (-0.142248368 + r * (0.7107068705 + r * (-0.7265760135 + r * 0.5307027145)))
    )
    tail = poly * bell
    cumulative = jnp.where(z >= 0.0, 1.0 - tail, tail)
    return z * cumulative, cumulative + z * (bell * DENSITY_SCALE)


def sizes(inputs_shape, hidden):
    s = types.SimpleNamespace()
    s.L, s.T = lax.axis_size("lon"), lax.axis_size("lat")
    s.R, s.W, s.C = inputs_shape[0], inputs_shape[1] // 2, inputs_shape[2]
    s.M = s.R * s.W
    s.HID = hidden
    s.CB = s.C // LANES
    assert s.CB * 2 == SUB
    s.I0 = 4 * s.CB
    s.WC = s.W * s.CB
    s.COLS = s.WC + 2 * s.I0
    s.ACC = s.WC + SUB
    s.PIECES = s.L * s.T
    s.CHUNK = hidden // s.PIECES
    s.CP = s.C // s.PIECES
    s.BN = max(s.CHUNK, 256)
    s.NB = hidden // s.BN
    s.K = 2 * s.T * s.M
    s.NP = 2 * s.L
    return s


def scratch_of(s):
    dma = pltpu.SemaphoreType.DMA
    vm = pltpu.VMEM
    return dict(
        nat=vm((6, s.R, s.W, s.C), BF16),
        p0=vm((4, s.R + 2 * MARGIN, s.COLS, LANES), F32),
        pb=vm((4, s.R + 2 * MARGIN, s.COLS, LANES), BF16),
        wt=vm((2, KERNEL * KERNEL * SUB, LANES), F32),
        a=vm((2, s.R, s.ACC, LANES), F32),
        ag=vm((2, s.R, s.ACC, LANES), F32),
        kg=vm((KERNEL * KERNEL * SUB, LANES), F32),
        tp=vm((2, KERNEL * KERNEL, s.C), BF16),
        vec=vm((2, 5, 1, s.C), F32),
        hbi=vm((2, 1, s.HID), F32),
        upw=vm((2, s.C, s.HID), BF16),
        dnw=vm((2, s.HID, s.C), BF16),
        un=vm((2, s.M, s.C), F32),
        inv=vm((2, s.M, LANES), F32),
        br=vm((2, s.M, s.C), F32),
        ng=vm((s.M, s.C), F32),
        sl=vm((2, s.NB, s.M, s.BN), F32),
        nrm=vm((s.M, s.C), BF16),
        scl=vm((2, s.M, s.C), BF16),
        hs=vm((2, s.T, s.L, s.M, s.CHUNK), BF16),
        bs=vm((2, s.T, s.L, s.M, s.CHUNK), BF16),
        nts=vm((2, s.C, s.M), BF16),
        sts=vm((2, s.C, s.M), BF16),
        hr=vm((s.L, s.K, s.CHUNK), BF16),
        bgr=vm((s.L, s.K, s.CHUNK), BF16),
        nr=vm((2 * s.T, s.C, s.M), BF16),
        sr=vm((2 * s.T, s.C, s.M), BF16),
        zs=vm((2, s.L, s.C, s.CHUNK), BF16),
        zm=vm((2, s.L, s.C, s.CHUNK), BF16),
        zr=vm((2, s.L // 2, s.C, s.CHUNK), BF16),
        zo=vm((2, s.C, s.CHUNK), F32),
        vs=vm((2, 5, 1, s.C), F32),
        sm=vm((2, SMALL_ROWS, s.C), F32),
        bh=vm((2, 1, s.HID), F32),
        sc=vm((2, s.PIECES, SMALL_ROWS // 2, 2 * s.CP), BF16),
        sib=vm((s.PIECES, SMALL_ROWS // 2, 2 * s.CP), BF16),
        scr=vm((s.PIECES, SMALL_ROWS // 2, 2 * s.CP), BF16),
        load=dma((4,)),
        prm_l=dma((7 + 2 * HALVES,)),
        prm_s=dma((7 + 2 * HALVES,)),
        prm_r=dma((7 + 2 * HALVES,)),
        halo_s=dma((4, 8)),
        halo_r=dma((4, 8)),
        f_s=dma((2, 4, s.T, s.L)),
        f_r=dma((4, 2 * s.T, s.L)),
        z_s=dma((2, s.L, 2)),
        zm_r=dma((2, s.L, 2)),
        z_r=dma((2, s.L // 2, 2)),
        s_s=dma((s.PIECES,)),
        s_r=dma((s.PIECES,)),
        o_s=dma((2, 2)),
        o_r=dma((2,)),
    )


def body(s, names, *refs):
    (x_in, g_in, k_in, cb_in, gain_in, shift_in, up_in, hb_in, dn_in, ob_in, ls_in) = refs[:11]
    so_out, bg_out, up_out, dn_out, hb_out, kg_out, vg_out = refs[11:18]
    v = types.SimpleNamespace(**dict(zip(names, refs[18:])))
    R, W, C, M, L, T, NP, CB = s.R, s.W, s.C, s.M, s.L, s.T, s.NP, s.CB
    c = lax.axis_index("segment")
    l = lax.axis_index("lon")
    t = lax.axis_index("lat")
    p = 2 * l + c
    north = t == 0
    south = t == T - 1

    def cell_at(place, row):
        return {"lat": row, "lon": place // 2, "segment": place % 2}

    def turn(place):
        return (place + NP) % NP

    own_cols = pl.ds(pl.multiple_of(c * W, W), W)
    load_x = pltpu.make_async_copy(x_in.at[:, own_cols, :], v.nat.at[0], v.load.at[0])
    load_g = pltpu.make_async_copy(g_in.at[:, own_cols, :], v.nat.at[3], v.load.at[1])
    load_x.start()
    load_g.start()
    params = [
        (k_in.at[0], v.tp.at[c]),
        (cb_in, v.vec.at[c, 0]),
        (gain_in, v.vec.at[c, 1]),
        (shift_in, v.vec.at[c, 2]),
        (ob_in, v.vec.at[c, 3]),
        (ls_in, v.vec.at[c, 4]),
        (hb_in, v.hbi.at[c]),
    ]
    width = s.HID // HALVES
    for h in range(HALVES):
        cols = pl.ds(h * width, width)
        params.append((up_in.at[0, :, cols], v.upw.at[c, :, cols]))
        params.append((dn_in.at[0, cols, :], v.dnw.at[c, cols, :]))
    local_params = [
        pltpu.make_async_copy(src, dst, v.prm_l.at[i]) for i, (src, dst) in enumerate(params)
    ]
    remote_params = [
        pltpu.make_async_remote_copy(
            src_ref=src,
            dst_ref=dst,
            send_sem=v.prm_s.at[i],
            recv_sem=v.prm_r.at[i],
            device_id={"segment": 1 - c},
            device_id_type=MESH,
        )
        for i, (src, dst) in enumerate(params)
    ]
    for copy in local_params:
        copy.start()

    barrier = pltpu.get_barrier_semaphore()
    for dl in range(L):
        for dt in range(T):
            for dc in range(2):
                if dl or dt or dc:
                    pl.semaphore_signal(
                        barrier,
                        inc=1,
                        device_id={
                            "lat": lax.rem(t + dt, T),
                            "lon": lax.rem(l + dl, L),
                            "segment": lax.rem(c + dc, 2),
                        },
                        device_id_type=MESH,
                    )

    mid = pl.ds(s.I0, s.WC)
    first_cols, last_cols = pl.ds(s.I0, s.I0), pl.ds(s.WC, s.I0)
    left_pad, right_pad = pl.ds(0, s.I0), pl.ds(s.I0 + s.WC, s.I0)
    top_rows, low_rows, own_rows = pl.ds(0, MARGIN), pl.ds(R + MARGIN, MARGIN), pl.ds(MARGIN, R)
    regions = [
        (top_rows, mid),
        (top_rows, left_pad),
        (top_rows, right_pad),
        (low_rows, mid),
        (low_rows, left_pad),
        (low_rows, right_pad),
        (own_rows, left_pad),
        (own_rows, right_pad),
    ]
    turned = NP // 2
    up_t, up_p = jnp.where(north, t, t - 1), jnp.where(north, p + turned, p)
    dn_t, dn_p = jnp.where(south, t, t + 1), jnp.where(south, p + turned, p)
    up_to, up_region = jnp.where(north, 0, R + MARGIN), jnp.where(north, 0, 3)
    dn_to, dn_region = jnp.where(south, R + MARGIN, 0), jnp.where(south, 3, 0)

    def halo_sends(n):
        head, tail = pl.ds(MARGIN, MARGIN), pl.ds(R, MARGIN)
        up_rows, dn_rows = pl.ds(up_to, MARGIN), pl.ds(dn_to, MARGIN)
        plans = [
            (own_rows, first_cols, own_rows, right_pad, 7, p - 1, t),
            (own_rows, last_cols, own_rows, left_pad, 6, p + 1, t),
            (head, mid, up_rows, mid, up_region, up_p, up_t),
            (tail, mid, dn_rows, mid, dn_region, dn_p, dn_t),
            (head, first_cols, up_rows, right_pad, up_region + 2, up_p - 1, up_t),
            (head, last_cols, up_rows, left_pad, up_region + 1, up_p + 1, up_t),
            (tail, first_cols, dn_rows, right_pad, dn_region + 2, dn_p - 1, dn_t),
            (tail, last_cols, dn_rows, left_pad, dn_region + 1, dn_p + 1, dn_t),
        ]
        return [
            pltpu.make_async_remote_copy(
                src_ref=v.pb.at[n, rows, cols],
                dst_ref=v.pb.at[n, to_rows, to_cols],
                send_sem=v.halo_s.at[n, i],
                recv_sem=v.halo_r.at[n, region],
                device_id=cell_at(turn(place), row),
                device_id_type=MESH,
            )
            for i, (rows, cols, to_rows, to_cols, region, place, row) in enumerate(plans)
        ]

    def region_wait(n, g):
        rows, cols = regions[g]
        spot = v.pb.at[n, rows, cols]
        pltpu.make_async_copy(spot, spot, v.halo_r.at[n, g]).wait()

    def wait_sides(n):
        region_wait(n, 6)
        region_wait(n, 7)

        def sides(i, carry):
            v.p0[n, i, left_pad] = v.pb[n, i, left_pad].astype(F32)
            v.p0[n, i, right_pad] = v.pb[n, i, right_pad].astype(F32)
            return carry

        lax.fori_loop(MARGIN, R + MARGIN, sides, 0)

    def wait_rows(n):
        for g in range(6):
            region_wait(n, g)
        for a in range(MARGIN):
            up_at = jnp.where(north, MARGIN - 1 - a, a)
            dn_at = R + MARGIN + jnp.where(south, MARGIN - 1 - a, a)
            v.p0[n, up_at] = v.pb[n, a].astype(F32)
            v.p0[n, dn_at] = v.pb[n, R + MARGIN + a].astype(F32)

    def write_row(n, i, value):
        row = i + MARGIN
        for b in range(CB):
            v.p0[n, row, pl.ds(s.I0 + b, W, stride=CB), :] = value[:, b * LANES : (b + 1) * LANES]
        v.pb[n, row, mid] = v.p0[n, row, mid].astype(BF16)

    def correlate(n, sec, backward):
        def weight(index):
            return v.wt[sec, pl.ds(pl.multiple_of(index * SUB, SUB), SUB), :]

        def tap(r, q):
            return (KERNEL * KERNEL - 1 if backward else 0) + (-1 if backward else 1) * (
                KERNEL * r + q
            )

        def edge_tap(r, q, pole):
            if backward:
                return jnp.where(pole, KERNEL * r + KERNEL - 1 - q, tap(r, q))
            return tap(r, q)

        def at_of(k, q):
            return pl.ds(pl.multiple_of(SUB * k + SUB * ((q + 1) // 2), SUB), SUB)

        wait_sides(n)
        for parity in range(2):
            col_taps = range(1 - parity, KERNEL, 2)

            def step(k, carry):
                total = jnp.zeros((R, SUB, LANES), F32)
                for q in col_taps:
                    rows = v.p0[n, own_rows, at_of(k, q), :]
                    for r in range(KERNEL):
                        low, high = max(0, MARGIN - r), min(R, R + MARGIN - r)
                        term = rows[low + r - MARGIN : high + r - MARGIN] * weight(tap(r, q))
                        middle = total[low:high] + term
                        if high < R:
                            total = jnp.concatenate([middle, total[high:]], axis=0)
                        elif low > 0:
                            total = jnp.concatenate([total[:low], middle], axis=0)
                        else:
                            total = middle
                v.a[parity, :, pl.ds(pl.multiple_of(SUB * k, SUB), SUB), :] = total
                return carry

            lax.fori_loop(0, s.WC // SUB + parity, step, 0)

        wait_rows(n)
        for parity in range(2):
            col_taps = range(1 - parity, KERNEL, 2)

            def step(k, carry):
                spot = pl.ds(pl.multiple_of(SUB * k, SUB), SUB)
                upper = v.a[parity, 0:MARGIN, spot, :]
                lower = v.a[parity, R - MARGIN : R, spot, :]
                for q in col_taps:
                    above = v.p0[n, top_rows, at_of(k, q), :]
                    below = v.p0[n, low_rows, at_of(k, q), :]
                    for r in range(MARGIN):
                        cut = MARGIN - r
                        part = upper[:cut] + above[r:] * weight(edge_tap(r, q, north))
                        upper = jnp.concatenate([part, upper[cut:]], axis=0) if r else part
                        far = KERNEL - 1 - r
                        part = lower[r:] + below[:cut] * weight(edge_tap(far, q, south))
                        lower = jnp.concatenate([lower[:r], part], axis=0) if r else part
                v.a[parity, 0:MARGIN, spot, :] = upper
                v.a[parity, R - MARGIN : R, spot, :] = lower
                return carry

            lax.fori_loop(0, s.WC // SUB + parity, step, 0)

    def correlated(i):
        return jnp.concatenate(
            [
                v.a[0, i, pl.ds(b, W, stride=CB), :] + v.a[1, i, pl.ds(CB + b, W, stride=CB), :]
                for b in range(CB)
            ],
            axis=1,
        )

    def stencil(n, sec):
        for q in range(KERNEL):
            parity = 1 - q % 2

            def step(k, totals):
                grad = v.ag[parity, :, pl.ds(pl.multiple_of(SUB * k, SUB), SUB), :]
                at = pl.multiple_of(SUB * k + SUB * ((q + 1) // 2), SUB)
                rows = v.p0[n, :, pl.ds(at, SUB), :]
                return tuple(
                    totals[r] + jnp.sum(rows[r : r + R] * grad, axis=0) for r in range(KERNEL)
                )

            zero = jnp.zeros((SUB, LANES), F32)
            totals = lax.fori_loop(0, s.WC // SUB + parity, step, (zero,) * KERNEL)
            for r in range(KERNEL):
                v.kg[pl.ds((KERNEL * r + q) * SUB, SUB), :] = totals[r]
        count = KERNEL * KERNEL
        for b in range(CB):
            v.sm[sec, 0:count, b * LANES : (b + 1) * LANES] = (
                v.kg[pl.ds(b, count, stride=SUB), :] + v.kg[pl.ds(CB + b, count, stride=SUB), :]
            )

    source = t * 2 + c
    place_k = pl.ds(pl.multiple_of(source * M, M), M)
    even = lax.rem(l, 2) == 0
    partner = l + 1 - 2 * lax.rem(l, 2)

    def z_to(i):
        to = jnp.where(even, L - 1 - i, i)
        beyond = jnp.where(even, to > l, to < l)
        return to, beyond

    def factor(kind, sec, dt, to):
        row = lax.rem(t + dt, T)
        if kind == 0:
            return v.hs.at[sec, row, to], v.hr.at[to, place_k, :]
        if kind == 1:
            return v.bs.at[sec, row, to], v.bgr.at[to, place_k, :]
        if kind == 2:
            return v.nts.at[sec], v.nr.at[source]
        return v.sts.at[sec], v.sr.at[source]

    def factor_remote(kind, sec, dt, to):
        src, dst = factor(kind, sec, dt, to)
        return pltpu.make_async_remote_copy(
            src_ref=src,
            dst_ref=dst,
            send_sem=v.f_s.at[sec, kind, dt, to],
            recv_sem=v.f_r.at[kind, source, to],
            device_id={"lat": lax.rem(t + dt, T), "segment": sec},
            device_id_type=MESH,
        )

    def factor_local(kind, sec, to):
        src, dst = factor(kind, sec, 0, to)
        return pltpu.make_async_copy(src, dst, v.f_r.at[kind, source, to])

    def send_factor(kind, sec):
        for i in range(L if kind < 2 else 1):
            to = z_to(i)[0] if kind < 2 else 0
            for dt in range(1, T):
                factor_remote(kind, sec, dt, to).start()

            @pl.when(c == sec)
            def _():
                factor_local(kind, sec, to).start()

            @pl.when(c != sec)
            def _():
                factor_remote(kind, sec, 0, to).start()

    def factor_done(kind, sec):
        for to in range(L if kind < 2 else 1):
            for dt in range(1, T):
                factor_remote(kind, sec, dt, to).wait_send()

            @pl.when(c != sec)
            def _():
                factor_remote(kind, sec, 0, to).wait_send()

    def factor_wait(kind, to):
        for d in range(2 * T):
            rows = pl.ds(d * M, M)
            if kind == 0:
                spot = v.hr.at[to, rows, :]
            elif kind == 1:
                spot = v.bgr.at[to, rows, :]
            else:
                spot = (v.nr if kind == 2 else v.sr).at[d]
            pltpu.make_async_copy(spot, spot, v.f_r.at[kind, d, to]).wait()

    def half(h):
        return pl.ds(h * (C // 2), C // 2)

    def z_merge(mat, to, h):
        return pltpu.make_async_remote_copy(
            src_ref=v.zs.at[mat, to, half(h)],
            dst_ref=v.zm.at[mat, to, half(h)],
            send_sem=v.z_s.at[mat, to, h],
            recv_sem=v.zm_r.at[mat, to, h],
            device_id={"lon": partner},
            device_id_type=MESH,
        )

    def z_final(mat, to, h):
        return pltpu.make_async_remote_copy(
            src_ref=v.zs.at[mat, to, half(h)],
            dst_ref=v.zr.at[mat, l // 2, half(h)],
            send_sem=v.z_s.at[mat, to, h],
            recv_sem=v.z_r.at[mat, l // 2, h],
            device_id={"lon": to},
            device_id_type=MESH,
        )

    def dense(sec, mat):
        @pl.when(c == sec)
        def _():
            left, right = (v.sr, v.hr) if mat == 0 else (v.nr, v.bgr)
            factor_wait(3 if mat == 0 else 2, 0)
            for i in range(L):
                to, beyond = z_to(i)
                factor_wait(0 if mat == 0 else 1, to)
                wide = jnp.concatenate([left[d] for d in range(2 * T)], axis=1)
                term = jnp.dot(wide, right[to], preferred_element_type=F32)

                @pl.when(beyond)
                def _():
                    v.zs[mat, to] = term.astype(BF16)

                    @pl.when(to == partner)
                    def _():
                        for h in range(2):
                            z_final(mat, to, h).start()

                    @pl.when(to != partner)
                    def _():
                        for h in range(2):
                            z_merge(mat, to, h).start()

                @pl.when(to == l)
                def _():
                    v.zo[mat] = term

                @pl.when(jnp.logical_not(jnp.logical_or(beyond, to == l)))
                def _():
                    v.zs[mat, to] = term.astype(BF16)

    def service(sec, mat):
        @pl.when(c == sec)
        def _():
            for i in range(L):
                to, beyond = z_to(i)

                @pl.when(jnp.logical_and(jnp.logical_not(beyond), to != l))
                def _():
                    for h in range(2):
                        z_merge(mat, to, h).wait_recv()
                        total = v.zs[mat, to, half(h)].astype(F32)
                        total = total + v.zm[mat, to, half(h)].astype(F32)
                        v.zs[mat, to, half(h)] = total.astype(BF16)
                        z_final(mat, to, h).start()

    def z_total(mat):
        total = v.zo[mat]
        for j in range(L // 2):
            for h in range(2):
                spot = v.zr.at[mat, j, half(h)]
                pltpu.make_async_copy(spot, spot, v.z_r.at[mat, j, h]).wait()
            total = total + v.zr[mat, j].astype(F32)
        return total

    def small_sibling(sec):
        return pltpu.make_async_remote_copy(
            src_ref=v.sc.at[sec],
            dst_ref=v.sib,
            send_sem=v.s_s.at[0],
            recv_sem=v.s_r.at[0],
            device_id={"segment": sec},
            device_id_type=MESH,
        )

    def small_remote(sec, dl, dt):
        to_l, to_t = lax.rem(l + dl, L), lax.rem(t + dt, T)
        return pltpu.make_async_remote_copy(
            src_ref=v.sc.at[sec, to_l * T + to_t],
            dst_ref=v.scr.at[dl * T + dt],
            send_sem=v.s_s.at[dl * T + dt],
            recv_sem=v.s_r.at[dl * T + dt],
            device_id={"lat": to_t, "lon": to_l},
            device_id_type=MESH,
        )

    taps = KERNEL * KERNEL
    bias_rows = s.HID // C
    away = [(dl, dt) for dl in range(L) for dt in range(T) if dl or dt]

    def send_small(sec):
        half_rows = SMALL_ROWS // 2
        for i in range(5):
            v.sm[sec, taps + i : taps + i + 1, :] = v.vs[sec, i]
        for piece in range(s.PIECES):
            rows = jnp.concatenate(
                [
                    v.bh[sec, :, piece * s.CHUNK + j * s.CP : piece * s.CHUNK + (j + 1) * s.CP]
                    for j in range(bias_rows)
                ]
                + [jnp.zeros((SUB - bias_rows, s.CP), F32)],
                axis=0,
            )
            block = v.sm[sec, :, piece * s.CP : (piece + 1) * s.CP]
            low = jnp.concatenate(
                [block[half_rows : SMALL_ROWS - SUB], block[SMALL_ROWS - SUB :] + rows], axis=0
            )
            v.sc[sec, piece] = jnp.concatenate([block[:half_rows], low], axis=1).astype(BF16)

        @pl.when(c != sec)
        def _():
            small_sibling(sec).start()

    def merge_small(sec):
        @pl.when(c == sec)
        def _():
            pltpu.make_async_copy(v.sib, v.sib, v.s_r.at[0]).wait()
            for piece in range(s.PIECES):
                total = v.sc[sec, piece].astype(F32) + v.sib[piece].astype(F32)
                v.sc[sec, piece] = total.astype(BF16)
            for dl, dt in away:
                small_remote(sec, dl, dt).start()

    def out_remote(kind, sec, source):
        out = so_out if kind == 0 else bg_out
        return pltpu.make_async_remote_copy(
            src_ref=source,
            dst_ref=out.at[:, own_cols, :],
            send_sem=v.o_s.at[kind, 1],
            recv_sem=v.o_r.at[kind],
            device_id={"segment": sec},
            device_id_type=MESH,
        )

    def out_local(kind, source):
        out = so_out if kind == 0 else bg_out
        return pltpu.make_async_copy(source, out.at[:, own_cols, :], v.o_s.at[kind, 0])

    def send_out(kind, sec, source):
        @pl.when(c == sec)
        def _():
            out_local(kind, source).start()

        @pl.when(c != sec)
        def _():
            out_remote(kind, sec, source).start()

    def vector(sec, which):
        return v.vec[sec, which]

    def wait_param(i, sec):
        @pl.when(c == sec)
        def _():
            local_params[i].wait()

        @pl.when(c != sec)
        def _():
            src, _ = params[i]
            spot = [v.tp.at[sec]] + [v.vec.at[sec, j] for j in range(5)]
            spot = spot + [v.hbi.at[sec]]
            for h in range(HALVES):
                cols = pl.ds(h * width, width)
                spot = spot + [v.upw.at[sec, :, cols], v.dnw.at[sec, cols, :]]
            spot = spot[i]
            pltpu.make_async_remote_copy(
                src_ref=spot,
                dst_ref=spot,
                send_sem=v.prm_s.at[i],
                recv_sem=v.prm_r.at[i],
                device_id={"segment": 1 - c},
                device_id_type=MESH,
            ).wait_recv()

    STEP = 2
    CELLS = STEP * W

    def block(ref, i):
        return jnp.concatenate([ref[i * STEP + j] for j in range(STEP)], axis=0)

    def cells(i):
        return pl.ds(pl.multiple_of(i * CELLS, CELLS), CELLS)

    def transpose_into(target, source):
        for b in range(CB):
            piece = source[:, b * LANES : (b + 1) * LANES].astype(F32)
            target[b * LANES : (b + 1) * LANES, :] = piece.T.astype(BF16)

    per = s.BN // s.CHUNK

    def scatter_pieces(ref, sec, b, value):
        for j in range(per):
            index = b * per + j
            ref[sec, lax.rem(index, T), index // T] = value[:, j * s.CHUNK : (j + 1) * s.CHUNK]

    def columns(b):
        return pl.ds(pl.multiple_of(b * s.BN, s.BN), s.BN)

    def forward(sec):
        correlate(sec, sec, False)

        def norm(i, carry):
            x = jnp.concatenate([correlated(i * STEP + j) for j in range(STEP)], axis=0)
            x = x + vector(sec, 0)
            mean = jnp.sum(x, axis=-1, keepdims=True) * (1.0 / C)
            x = x - mean
            var = jnp.sum(x * x, axis=-1, keepdims=True) * (1.0 / C)
            inv = lax.rsqrt(var + EPSILON)
            unit = x * inv
            v.un[sec, cells(i), :] = unit
            v.inv[sec, cells(i), :] = jnp.broadcast_to(inv, (CELLS, LANES))
            v.nrm[cells(i), :] = (unit * vector(sec, 1) + vector(sec, 2)).astype(BF16)
            return carry

        lax.fori_loop(0, R // STEP, norm, 0)
        transpose_into(v.nts.at[sec], v.nrm)
        if sec == 1:
            send_factor(2, 1)
        v.br[sec] = jnp.broadcast_to(vector(sec, 3), (M, C))

        def hidden_block(b, carry):
            before = (
                jnp.dot(v.nrm[...], v.upw[sec, :, columns(b)], preferred_element_type=F32)
                + v.hbi[sec, :, columns(b)]
            )
            active, slope = gelu_parts(before)
            v.sl[sec, b] = slope
            active = active.astype(BF16)
            scatter_pieces(v.hs, sec, b, active)
            v.br[sec] += jnp.dot(active, v.dnw[sec, columns(b), :], preferred_element_type=F32)
            return carry

        step = s.NB // HALVES
        for h in range(HALVES):
            wait_param(7 + 2 * h, sec)
            wait_param(8 + 2 * h, sec)
            lax.fori_loop(h * step, (h + 1) * step, hidden_block, 0, unroll=True)

        def finish(i, carry):
            u = block(v.nat.at[sec], i).astype(F32)
            u = (u + vector(sec, 4) * v.br[sec, cells(i), :]).astype(BF16)
            for j in range(STEP):
                row = u[j * W : (j + 1) * W]
                v.nat[sec + 1, i * STEP + j] = row
                if sec == 0:
                    write_row(1, i * STEP + j, row.astype(F32))
            return carry

        lax.fori_loop(0, R // STEP, finish, 0)

    def scale(sec, at):
        def rows(i, carry):
            g = block(v.nat.at[at], i).astype(F32)
            low = (g * vector(sec, 4)).astype(BF16)
            v.scl[sec, cells(i), :] = low
            return carry + jnp.sum(low.astype(F32), axis=0, keepdims=True)

        v.vs[sec, 3] = lax.fori_loop(0, R // STEP, rows, jnp.zeros((1, C), F32))
        transpose_into(v.sts.at[sec], v.scl.at[sec])

    def branch_sum(sec, at):
        def rows(i, carry):
            g = block(v.nat.at[at], i).astype(F32)
            return carry + jnp.sum(g * v.br[sec, cells(i), :], axis=0, keepdims=True)

        v.vs[sec, 4] = lax.fori_loop(0, R // STEP, rows, jnp.zeros((1, C), F32))

    def backward(sec, n):
        v.ng[...] = jnp.zeros((M, C), F32)

        def hidden_block(b, carry):
            grad = lax.dot_general(
                v.scl[sec], v.dnw[sec, columns(b), :], CONTRACT_LAST, preferred_element_type=F32
            )
            low = (grad * v.sl[sec, b]).astype(BF16)
            scatter_pieces(v.bs, sec, b, low)
            v.bh[sec, :, columns(b)] = jnp.sum(low.astype(F32), axis=0, keepdims=True)
            v.ng[...] += lax.dot_general(
                low, v.upw[sec, :, columns(b)], CONTRACT_LAST, preferred_element_type=F32
            )
            return carry

        lax.fori_loop(0, s.NB, hidden_block, 0, unroll=True)

        def norm(i, carry):
            bias_sum, gain_sum, shift_sum = carry
            ng = v.ng[cells(i), :]
            unit = v.un[sec, cells(i), :]
            inv = v.inv[sec, cells(i), :][:, :1]
            both = ng * unit
            gained = ng * vector(sec, 1)
            mean = jnp.sum(gained, axis=-1, keepdims=True) * (1.0 / C)
            along = jnp.sum(gained * unit, axis=-1, keepdims=True) * (1.0 / C)
            grad = (inv * (gained - mean - unit * along)).astype(BF16).astype(F32)
            for j in range(STEP):
                row = grad[j * W : (j + 1) * W]
                write_row(n, i * STEP + j, row)
                for b in range(CB):
                    lanes = row[:, b * LANES : (b + 1) * LANES]
                    v.ag[0, i * STEP + j, pl.ds(b, W, stride=CB), :] = lanes
                    v.ag[1, i * STEP + j, pl.ds(CB + b, W, stride=CB), :] = lanes
            return (
                bias_sum + jnp.sum(grad, axis=0, keepdims=True),
                gain_sum + jnp.sum(both, axis=0, keepdims=True),
                shift_sum + jnp.sum(ng, axis=0, keepdims=True),
            )

        zero = jnp.zeros((1, C), F32)
        totals = lax.fori_loop(0, R // STEP, norm, (zero, zero, zero))
        for i in range(3):
            v.vs[sec, i] = totals[i]

    def through(sec, n, at, to):
        correlate(n, sec, True)

        def rows(i, carry):
            g = v.nat[at, i].astype(F32)
            v.nat[to, i] = (g + correlated(i)).astype(BF16)
            return carry

        lax.fori_loop(0, R, rows, 0)

    load_x.wait()

    def first_rows(i, carry):
        write_row(0, i, v.nat[0, i].astype(F32))
        return carry

    lax.fori_loop(0, R, first_rows, 0)
    for sec in range(2):
        v.sm[sec] = jnp.zeros((SMALL_ROWS, C), F32)
    for i in range(R):
        v.ag[0, i, s.WC : s.ACC] = jnp.zeros((SUB, LANES), F32)
        v.ag[1, i, 0:SUB] = jnp.zeros((SUB, LANES), F32)
        v.ag[1, i, s.WC : s.ACC] = jnp.zeros((SUB, LANES), F32)
    pl.semaphore_wait(barrier, 2 * L * T - 1)
    for copy in halo_sends(0) + remote_params:
        copy.start()
    for sec in range(2):
        for i in range(7):
            wait_param(i, sec)
        for b in range(CB):
            piece = v.tp[sec, :, b * LANES : (b + 1) * LANES].astype(F32)
            v.wt[sec, pl.ds(b, taps, stride=SUB), :] = piece
            v.wt[sec, pl.ds(CB + b, taps, stride=SUB), :] = piece
    load_g.wait()
    scale(1, 3)
    send_factor(3, 1)

    forward(0)
    for copy in halo_sends(1):
        copy.start()
    send_factor(0, 0)
    send_out(0, 0, v.nat.at[1])

    forward(1)
    send_factor(0, 1)
    backward(1, 2)
    for copy in halo_sends(2):
        copy.start()
    send_factor(1, 1)
    send_out(0, 1, v.nat.at[2])
    stencil(1, 1)
    branch_sum(1, 3)
    dense(1, 0)

    through(1, 2, 3, 4)
    scale(0, 4)
    send_factor(3, 0)
    send_factor(2, 0)
    backward(0, 3)
    for copy in halo_sends(3):
        copy.start()
    send_factor(1, 0)
    service(1, 0)
    dense(1, 1)
    dense(0, 0)
    send_out(1, 1, v.nat.at[4])
    branch_sum(0, 4)
    send_small(1)
    stencil(0, 0)
    send_small(0)
    merge_small(1)
    service(1, 1)
    merge_small(0)
    service(0, 0)
    dense(0, 1)
    through(0, 3, 4, 5)
    send_out(1, 0, v.nat.at[5])
    service(0, 1)

    sums = v.sc[c, l * T + t].astype(F32)
    for dl, dt in away:
        spot = v.scr.at[dl * T + dt]
        pltpu.make_async_copy(spot, spot, v.s_r.at[dl * T + dt]).wait()
        sums = sums + v.scr[dl * T + dt].astype(F32)
    total = jnp.concatenate([sums[:, : s.CP], sums[:, s.CP :]], axis=0)
    for i in range(taps):
        kg_out[i] = total[i : i + 1]
    for i in range(5):
        vg_out[i] = total[taps + i : taps + i + 1]
    for j in range(bias_rows):
        row = SMALL_ROWS - SUB + j
        hb_out[:, j * s.CP : (j + 1) * s.CP] = total[row : row + 1]
    dn_out[...] = z_total(0).T
    up_out[...] = z_total(1)

    for kind in range(2):
        any_half = v.nat.at[0]

        @pl.when(c == 0)
        def _():
            out_remote(kind, 1, any_half).wait_send()
            out_local(kind, any_half).wait()

        @pl.when(c == 1)
        def _():
            out_remote(kind, 0, any_half).wait_send()
            out_local(kind, any_half).wait()

        out = so_out if kind == 0 else bg_out
        spot = out.at[:, pl.ds(pl.multiple_of((1 - c) * W, W), W), :]
        pltpu.make_async_remote_copy(
            src_ref=spot,
            dst_ref=spot,
            send_sem=v.o_s.at[kind, 1],
            recv_sem=v.o_r.at[kind],
            device_id={"segment": 1 - c},
            device_id_type=MESH,
        ).wait_recv()
    for copy in remote_params:
        copy.wait_send()
    for n in range(4):
        for copy in halo_sends(n):
            copy.wait_send()
    for sec in range(2):
        for kind in range(4):
            factor_done(kind, sec)
    small_sibling(1 - c).wait_send()
    for dl, dt in away:
        small_remote(c, dl, dt).wait_send()
    for mat in range(2):
        for i in range(L):

            @pl.when(i != l)
            def _():
                for h in range(2):
                    z_final(mat, i, h).wait_send()


def hand_out(*refs):
    count = len(refs) // 2
    for i in range(count):
        refs[count + i][...] = refs[i][...]


def local(*args):
    inputs, up_weight = args[0], args[6]
    s = sizes(inputs.shape, up_weight.shape[2])
    scratch = scratch_of(s)
    full = pl.BlockSpec(memory_space=pltpu.VMEM)
    hbm = pl.BlockSpec(memory_space=pl.ANY)
    results = (
        pl.pallas_call(
            functools.partial(body, s, tuple(scratch)),
            out_shape=[
                jax.ShapeDtypeStruct(inputs.shape, BF16),
                jax.ShapeDtypeStruct(inputs.shape, BF16),
                jax.ShapeDtypeStruct((s.C, s.CHUNK), F32),
                jax.ShapeDtypeStruct((s.CHUNK, s.C), F32),
                jax.ShapeDtypeStruct((1, s.CHUNK), F32),
                jax.ShapeDtypeStruct((KERNEL * KERNEL, 1, s.CP), F32),
                jax.ShapeDtypeStruct((5, 1, s.CP), F32),
            ],
            in_specs=[hbm] * len(args),
            out_specs=[hbm, hbm] + [full] * 5,
            scratch_shapes=list(scratch.values()),
            compiler_params=pltpu.CompilerParams(
                collective_id=0, has_side_effects=True, vmem_limit_bytes=58 * 1024 * 1024
            ),
        )(*args)
    )
    section_out, boundary_grad, up_grad, down_grad, bias_grad, kernel_grad, vector_grad = (
        pl.pallas_call(
            hand_out,
            out_shape=[jax.ShapeDtypeStruct(x.shape, x.dtype) for x in results],
            in_specs=[full] * len(results),
            out_specs=[full] * len(results),
        )(*results)
    )
    return (
        section_out[None],
        boundary_grad[None],
        up_grad[None],
        down_grad[None],
        bias_grad,
        kernel_grad.transpose(1, 0, 2),
        vector_grad.transpose(1, 0, 2),
    )


def solution(mesh):
    placed = (
        P(("groups", "lat"), "lon", None),
        P(("groups", "lat"), "lon", None),
        P("segment", None, None),
        P("segment", None),
        P("segment", None),
        P("segment", None),
        P("segment", None, None),
        P("segment", None),
        P("segment", None, None),
        P("segment", None),
        P("segment", None),
    )
    return jax.shard_map(
        local,
        mesh=mesh,
        in_specs=placed,
        out_specs=(
            P("segment", ("groups", "lat"), "lon", None),
            P("segment", ("groups", "lat"), "lon", None),
            P(("groups", "segment"), None, ("lon", "lat")),
            P(("groups", "segment"), ("lon", "lat"), None),
            P(("groups", "segment"), ("lon", "lat")),
            P(("groups", "segment"), None, ("lon", "lat")),
            P(("groups", "segment"), None, ("lon", "lat")),
        ),
        check_vma=False,
    )
```

```python
import functools
import types
import jax
import jax.numpy as jnp
from jax import lax
from jax.experimental import pallas as pl
from jax.experimental.pallas import tpu as pltpu
from jax.sharding import PartitionSpec as P

KERNEL = 7
MARGIN = KERNEL // 2
EPSILON = 1e-06
ROOT_HALF = 0.7071067811865476
DENSITY_SCALE = 0.3989422804014327
LANES = 128
SUB = 8
MESH = pl.DeviceIdType.MESH
F32 = jnp.float32
BF16 = jnp.bfloat16
CONTRACT_LAST = (((1,), (1,)), ((), ()))
SMALL_ROWS = 64
HALVES = 1


def gelu_parts(z):
    bell = jnp.exp(-0.5 * z * z)
    d = 1.0 + (0.3275911 * ROOT_HALF) * jnp.abs(z)
    r = pl.reciprocal(d, approx=True)
    r = r * (2.0 - d * r)
    poly = r * (
        0.127414796
        + r * (-0.142248368 + r * (0.7107068705 + r * (-0.7265760135 + r * 0.5307027145)))
    )
    tail = poly * bell
    cumulative = jnp.where(z >= 0.0, 1.0 - tail, tail)
    return z * cumulative, cumulative + z * (bell * DENSITY_SCALE)


def sizes(inputs_shape, hidden):
    s = types.SimpleNamespace()
    s.L, s.T = lax.axis_size("lon"), lax.axis_size("lat")
    s.R, s.W, s.C = inputs_shape[0], inputs_shape[1] // 2, inputs_shape[2]
    s.M = s.R * s.W
    s.HID = hidden
    s.CB = s.C // LANES
    assert s.CB * 2 == SUB
    s.I0 = 4 * s.CB
    s.WC = s.W * s.CB
    s.COLS = s.WC + 2 * s.I0
    s.ACC = s.WC + SUB
    s.PIECES = s.L * s.T
    s.CHUNK = hidden // s.PIECES
    s.CP = s.C // s.PIECES
    s.BN = max(s.CHUNK, 256)
    s.NB = hidden // s.BN
    s.K = 2 * s.T * s.M
    s.NP = 2 * s.L
    return s


def scratch_of(s):
    dma = pltpu.SemaphoreType.DMA
    vm = pltpu.VMEM
    return dict(
        nat=vm((6, s.R, s.W, s.C), BF16),
        p0=vm((4, s.R + 2 * MARGIN, s.COLS, LANES), F32),
        pb=vm((4, s.R + 2 * MARGIN, s.COLS, LANES), BF16),
        wt=vm((2, KERNEL * KERNEL * SUB, LANES), F32),
        a=vm((2, s.R, s.ACC, LANES), F32),
        ag=vm((2, s.R, s.ACC, LANES), F32),
        kg=vm((KERNEL * KERNEL * SUB, LANES), F32),
        tp=vm((2, KERNEL * KERNEL, s.C), BF16),
        vec=vm((2, 5, 1, s.C), F32),
        hbi=vm((2, 1, s.HID), F32),
        upw=vm((2, s.C, s.HID), BF16),
        dnw=vm((2, s.HID, s.C), BF16),
        un=vm((2, s.M, s.C), F32),
        inv=vm((2, s.M, LANES), F32),
        br=vm((2, s.M, s.C), F32),
        ng=vm((s.M, s.C), F32),
        sl=vm((2, s.NB, s.M, s.BN), F32),
        nrm=vm((s.M, s.C), BF16),
        scl=vm((2, s.M, s.C), BF16),
        hs=vm((2, s.T, s.L, s.M, s.CHUNK), BF16),
        bs=vm((2, s.T, s.L, s.M, s.CHUNK), BF16),
        nts=vm((2, s.C, s.M), BF16),
        sts=vm((2, s.C, s.M), BF16),
        hr=vm((s.L, s.K, s.CHUNK), BF16),
        bgr=vm((s.L, s.K, s.CHUNK), BF16),
        nr=vm((2 * s.T, s.C, s.M), BF16),
        sr=vm((2 * s.T, s.C, s.M), BF16),
        zs=vm((2, s.L, s.C, s.CHUNK), BF16),
        zm=vm((2, s.L, s.C, s.CHUNK), BF16),
        zr=vm((2, s.L // 2, s.C, s.CHUNK), BF16),
        zo=vm((2, s.C, s.CHUNK), F32),
        vs=vm((2, 5, 1, s.C), F32),
        sm=vm((2, SMALL_ROWS, s.C), F32),
        bh=vm((2, 1, s.HID), F32),
        sc=vm((2, s.PIECES, SMALL_ROWS // 2, 2 * s.CP), BF16),
        sib=vm((s.PIECES, SMALL_ROWS // 2, 2 * s.CP), BF16),
        scr=vm((s.PIECES, SMALL_ROWS // 2, 2 * s.CP), BF16),
        load=dma((4,)),
        prm_l=dma((7 + 2 * HALVES,)),
        prm_s=dma((7 + 2 * HALVES,)),
        prm_r=dma((7 + 2 * HALVES,)),
        halo_s=dma((4, 8)),
        halo_r=dma((4, 8)),
        f_s=dma((2, 4, s.T, s.L)),
        f_r=dma((4, 2 * s.T, s.L)),
        z_s=dma((2, s.L, 2)),
        zm_r=dma((2, s.L, 2)),
        z_r=dma((2, s.L // 2, 2)),
        s_s=dma((s.PIECES,)),
        s_r=dma((s.PIECES,)),
        o_s=dma((2, 2)),
        o_r=dma((2,)),
    )


def body(s, names, *refs):
    (x_in, g_in, k_in, cb_in, gain_in, shift_in, up_in, hb_in, dn_in, ob_in, ls_in) = refs[:11]
    so_out, bg_out, up_out, dn_out, hb_out, kg_out, vg_out = refs[11:18]
    v = types.SimpleNamespace(**dict(zip(names, refs[18:])))
    R, W, C, M, L, T, NP, CB = s.R, s.W, s.C, s.M, s.L, s.T, s.NP, s.CB
    c = lax.axis_index("segment")
    l = lax.axis_index("lon")
    t = lax.axis_index("lat")
    p = 2 * l + c
    north = t == 0
    south = t == T - 1

    def cell_at(place, row):
        return {"lat": row, "lon": place // 2, "segment": place % 2}

    def turn(place):
        return (place + NP) % NP

    own_cols = pl.ds(pl.multiple_of(c * W, W), W)
    load_x = pltpu.make_async_copy(x_in.at[:, own_cols, :], v.nat.at[0], v.load.at[0])
    load_g = pltpu.make_async_copy(g_in.at[:, own_cols, :], v.nat.at[3], v.load.at[1])
    load_x.start()
    load_g.start()
    params = [
        (k_in.at[0], v.tp.at[c]),
        (cb_in, v.vec.at[c, 0]),
        (gain_in, v.vec.at[c, 1]),
        (shift_in, v.vec.at[c, 2]),
        (ob_in, v.vec.at[c, 3]),
        (ls_in, v.vec.at[c, 4]),
        (hb_in, v.hbi.at[c]),
    ]
    width = s.HID // HALVES
    for h in range(HALVES):
        cols = pl.ds(h * width, width)
        params.append((up_in.at[0, :, cols], v.upw.at[c, :, cols]))
        params.append((dn_in.at[0, cols, :], v.dnw.at[c, cols, :]))
    local_params = [
        pltpu.make_async_copy(src, dst, v.prm_l.at[i]) for i, (src, dst) in enumerate(params)
    ]
    remote_params = [
        pltpu.make_async_remote_copy(
            src_ref=src,
            dst_ref=dst,
            send_sem=v.prm_s.at[i],
            recv_sem=v.prm_r.at[i],
            device_id={"segment": 1 - c},
            device_id_type=MESH,
        )
        for i, (src, dst) in enumerate(params)
    ]
    for copy in local_params:
        copy.start()

    barrier = pltpu.get_barrier_semaphore()
    for dl in range(L):
        for dt in range(T):
            for dc in range(2):
                if dl or dt or dc:
                    pl.semaphore_signal(
                        barrier,
                        inc=1,
                        device_id={
                            "lat": lax.rem(t + dt, T),
                            "lon": lax.rem(l + dl, L),
                            "segment": lax.rem(c + dc, 2),
                        },
                        device_id_type=MESH,
                    )

    mid = pl.ds(s.I0, s.WC)
    first_cols, last_cols = pl.ds(s.I0, s.I0), pl.ds(s.WC, s.I0)
    left_pad, right_pad = pl.ds(0, s.I0), pl.ds(s.I0 + s.WC, s.I0)
    top_rows, low_rows, own_rows = pl.ds(0, MARGIN), pl.ds(R + MARGIN, MARGIN), pl.ds(MARGIN, R)
    regions = [
        (top_rows, mid),
        (top_rows, left_pad),
        (top_rows, right_pad),
        (low_rows, mid),
        (low_rows, left_pad),
        (low_rows, right_pad),
        (own_rows, left_pad),
        (own_rows, right_pad),
    ]
    turned = NP // 2
    up_t, up_p = jnp.where(north, t, t - 1), jnp.where(north, p + turned, p)
    dn_t, dn_p = jnp.where(south, t, t + 1), jnp.where(south, p + turned, p)
    up_to, up_region = jnp.where(north, 0, R + MARGIN), jnp.where(north, 0, 3)
    dn_to, dn_region = jnp.where(south, R + MARGIN, 0), jnp.where(south, 3, 0)

    def halo_sends(n):
        head, tail = pl.ds(MARGIN, MARGIN), pl.ds(R, MARGIN)
        up_rows, dn_rows = pl.ds(up_to, MARGIN), pl.ds(dn_to, MARGIN)
        plans = [
            (own_rows, first_cols, own_rows, right_pad, 7, p - 1, t),
            (own_rows, last_cols, own_rows, left_pad, 6, p + 1, t),
            (head, mid, up_rows, mid, up_region, up_p, up_t),
            (tail, mid, dn_rows, mid, dn_region, dn_p, dn_t),
            (head, first_cols, up_rows, right_pad, up_region + 2, up_p - 1, up_t),
            (head, last_cols, up_rows, left_pad, up_region + 1, up_p + 1, up_t),
            (tail, first_cols, dn_rows, right_pad, dn_region + 2, dn_p - 1, dn_t),
            (tail, last_cols, dn_rows, left_pad, dn_region + 1, dn_p + 1, dn_t),
        ]
        return [
            pltpu.make_async_remote_copy(
                src_ref=v.pb.at[n, rows, cols],
                dst_ref=v.pb.at[n, to_rows, to_cols],
                send_sem=v.halo_s.at[n, i],
                recv_sem=v.halo_r.at[n, region],
                device_id=cell_at(turn(place), row),
                device_id_type=MESH,
            )
            for i, (rows, cols, to_rows, to_cols, region, place, row) in enumerate(plans)
        ]

    def region_wait(n, g):
        rows, cols = regions[g]
        spot = v.pb.at[n, rows, cols]
        pltpu.make_async_copy(spot, spot, v.halo_r.at[n, g]).wait()

    def wait_sides(n):
        region_wait(n, 6)
        region_wait(n, 7)

        def sides(i, carry):
            v.p0[n, i, left_pad] = v.pb[n, i, left_pad].astype(F32)
            v.p0[n, i, right_pad] = v.pb[n, i, right_pad].astype(F32)
            return carry

        lax.fori_loop(MARGIN, R + MARGIN, sides, 0)

    def wait_rows(n):
        for g in range(6):
            region_wait(n, g)
        for a in range(MARGIN):
            up_at = jnp.where(north, MARGIN - 1 - a, a)
            dn_at = R + MARGIN + jnp.where(south, MARGIN - 1 - a, a)
            v.p0[n, up_at] = v.pb[n, a].astype(F32)
            v.p0[n, dn_at] = v.pb[n, R + MARGIN + a].astype(F32)

    def write_row(n, i, value):
        row = i + MARGIN
        for b in range(CB):
            v.p0[n, row, pl.ds(s.I0 + b, W, stride=CB), :] = value[:, b * LANES : (b + 1) * LANES]
        v.pb[n, row, mid] = v.p0[n, row, mid].astype(BF16)

    def correlate(n, sec, backward):
        def weight(index):
            return v.wt[sec, pl.ds(pl.multiple_of(index * SUB, SUB), SUB), :]

        def tap(r, q):
            return (KERNEL * KERNEL - 1 if backward else 0) + (-1 if backward else 1) * (
                KERNEL * r + q
            )

        def edge_tap(r, q, pole):
            if backward:
                return jnp.where(pole, KERNEL * r + KERNEL - 1 - q, tap(r, q))
            return tap(r, q)

        def at_of(k, q):
            return pl.ds(pl.multiple_of(SUB * k + SUB * ((q + 1) // 2), SUB), SUB)

        wait_sides(n)
        for parity in range(2):
            col_taps = range(1 - parity, KERNEL, 2)

            def step(k, carry):
                total = jnp.zeros((R, SUB, LANES), F32)
                for q in col_taps:
                    rows = v.p0[n, own_rows, at_of(k, q), :]
                    for r in range(KERNEL):
                        low, high = max(0, MARGIN - r), min(R, R + MARGIN - r)
                        term = rows[low + r - MARGIN : high + r - MARGIN] * weight(tap(r, q))
                        middle = total[low:high] + term
                        if high < R:
                            total = jnp.concatenate([middle, total[high:]], axis=0)
                        elif low > 0:
                            total = jnp.concatenate([total[:low], middle], axis=0)
                        else:
                            total = middle
                v.a[parity, :, pl.ds(pl.multiple_of(SUB * k, SUB), SUB), :] = total
                return carry

            lax.fori_loop(0, s.WC // SUB + parity, step, 0)

        wait_rows(n)
        for parity in range(2):
            col_taps = range(1 - parity, KERNEL, 2)

            def step(k, carry):
                spot = pl.ds(pl.multiple_of(SUB * k, SUB), SUB)
                upper = v.a[parity, 0:MARGIN, spot, :]
                lower = v.a[parity, R - MARGIN : R, spot, :]
                for q in col_taps:
                    above = v.p0[n, top_rows, at_of(k, q), :]
                    below = v.p0[n, low_rows, at_of(k, q), :]
                    for r in range(MARGIN):
                        cut = MARGIN - r
                        part = upper[:cut] + above[r:] * weight(edge_tap(r, q, north))
                        upper = jnp.concatenate([part, upper[cut:]], axis=0) if r else part
                        far = KERNEL - 1 - r
                        part = lower[r:] + below[:cut] * weight(edge_tap(far, q, south))
                        lower = jnp.concatenate([lower[:r], part], axis=0) if r else part
                v.a[parity, 0:MARGIN, spot, :] = upper
                v.a[parity, R - MARGIN : R, spot, :] = lower
                return carry

            lax.fori_loop(0, s.WC // SUB + parity, step, 0)

    def correlated(i):
        return jnp.concatenate(
            [
                v.a[0, i, pl.ds(b, W, stride=CB), :] + v.a[1, i, pl.ds(CB + b, W, stride=CB), :]
                for b in range(CB)
            ],
            axis=1,
        )

    def stencil(n, sec):
        for q in range(KERNEL):
            parity = 1 - q % 2

            def step(k, totals):
                grad = v.ag[parity, :, pl.ds(pl.multiple_of(SUB * k, SUB), SUB), :]
                at = pl.multiple_of(SUB * k + SUB * ((q + 1) // 2), SUB)
                rows = v.p0[n, :, pl.ds(at, SUB), :]
                return tuple(
                    totals[r] + jnp.sum(rows[r : r + R] * grad, axis=0) for r in range(KERNEL)
                )

            zero = jnp.zeros((SUB, LANES), F32)
            totals = lax.fori_loop(0, s.WC // SUB + parity, step, (zero,) * KERNEL)
            for r in range(KERNEL):
                v.kg[pl.ds((KERNEL * r + q) * SUB, SUB), :] = totals[r]
        count = KERNEL * KERNEL
        for b in range(CB):
            v.sm[sec, 0:count, b * LANES : (b + 1) * LANES] = (
                v.kg[pl.ds(b, count, stride=SUB), :] + v.kg[pl.ds(CB + b, count, stride=SUB), :]
            )

    source = t * 2 + c
    place_k = pl.ds(pl.multiple_of(source * M, M), M)
    even = lax.rem(l, 2) == 0
    partner = l + 1 - 2 * lax.rem(l, 2)

    def z_to(i):
        to = jnp.where(even, L - 1 - i, i)
        beyond = jnp.where(even, to > l, to < l)
        return to, beyond

    def factor(kind, sec, dt, to):
        row = lax.rem(t + dt, T)
        if kind == 0:
            return v.hs.at[sec, row, to], v.hr.at[to, place_k, :]
        if kind == 1:
            return v.bs.at[sec, row, to], v.bgr.at[to, place_k, :]
        if kind == 2:
            return v.nts.at[sec], v.nr.at[source]
        return v.sts.at[sec], v.sr.at[source]

    def factor_remote(kind, sec, dt, to):
        src, dst = factor(kind, sec, dt, to)
        return pltpu.make_async_remote_copy(
            src_ref=src,
            dst_ref=dst,
            send_sem=v.f_s.at[sec, kind, dt, to],
            recv_sem=v.f_r.at[kind, source, to],
            device_id={"lat": lax.rem(t + dt, T), "segment": sec},
            device_id_type=MESH,
        )

    def factor_local(kind, sec, to):
        src, dst = factor(kind, sec, 0, to)
        return pltpu.make_async_copy(src, dst, v.f_r.at[kind, source, to])

    def send_factor(kind, sec):
        for i in range(L if kind < 2 else 1):
            to = z_to(i)[0] if kind < 2 else 0
            for dt in range(1, T):
                factor_remote(kind, sec, dt, to).start()

            @pl.when(c == sec)
            def _():
                factor_local(kind, sec, to).start()

            @pl.when(c != sec)
            def _():
                factor_remote(kind, sec, 0, to).start()

    def factor_done(kind, sec):
        for to in range(L if kind < 2 else 1):
            for dt in range(1, T):
                factor_remote(kind, sec, dt, to).wait_send()

            @pl.when(c != sec)
            def _():
                factor_remote(kind, sec, 0, to).wait_send()

    def factor_wait(kind, to):
        for d in range(2 * T):
            rows = pl.ds(d * M, M)
            if kind == 0:
                spot = v.hr.at[to, rows, :]
            elif kind == 1:
                spot = v.bgr.at[to, rows, :]
            else:
                spot = (v.nr if kind == 2 else v.sr).at[d]
            pltpu.make_async_copy(spot, spot, v.f_r.at[kind, d, to]).wait()

    def half(h):
        return pl.ds(h * (C // 2), C // 2)

    def z_merge(mat, to, h):
        return pltpu.make_async_remote_copy(
            src_ref=v.zs.at[mat, to, half(h)],
            dst_ref=v.zm.at[mat, to, half(h)],
            send_sem=v.z_s.at[mat, to, h],
            recv_sem=v.zm_r.at[mat, to, h],
            device_id={"lon": partner},
            device_id_type=MESH,
        )

    def z_final(mat, to, h):
        return pltpu.make_async_remote_copy(
            src_ref=v.zs.at[mat, to, half(h)],
            dst_ref=v.zr.at[mat, l // 2, half(h)],
            send_sem=v.z_s.at[mat, to, h],
            recv_sem=v.z_r.at[mat, l // 2, h],
            device_id={"lon": to},
            device_id_type=MESH,
        )

    def dense(sec, mat):
        @pl.when(c == sec)
        def _():
            left, right = (v.sr, v.hr) if mat == 0 else (v.nr, v.bgr)
            factor_wait(3 if mat == 0 else 2, 0)
            for i in range(L):
                to, beyond = z_to(i)
                factor_wait(0 if mat == 0 else 1, to)
                wide = jnp.concatenate([left[d] for d in range(2 * T)], axis=1)
                term = jnp.dot(wide, right[to], preferred_element_type=F32)

                @pl.when(beyond)
                def _():
                    v.zs[mat, to] = term.astype(BF16)

                    @pl.when(to == partner)
                    def _():
                        for h in range(2):
                            z_final(mat, to, h).start()

                    @pl.when(to != partner)
                    def _():
                        for h in range(2):
                            z_merge(mat, to, h).start()

                @pl.when(to == l)
                def _():
                    v.zo[mat] = term

                @pl.when(jnp.logical_not(jnp.logical_or(beyond, to == l)))
                def _():
                    v.zs[mat, to] = term.astype(BF16)

    def service(sec, mat):
        @pl.when(c == sec)
        def _():
            for i in range(L):
                to, beyond = z_to(i)

                @pl.when(jnp.logical_and(jnp.logical_not(beyond), to != l))
                def _():
                    for h in range(2):
                        z_merge(mat, to, h).wait_recv()
                        total = v.zs[mat, to, half(h)].astype(F32)
                        total = total + v.zm[mat, to, half(h)].astype(F32)
                        v.zs[mat, to, half(h)] = total.astype(BF16)
                        z_final(mat, to, h).start()

    def z_total(mat):
        total = v.zo[mat]
        for j in range(L // 2):
            for h in range(2):
                spot = v.zr.at[mat, j, half(h)]
                pltpu.make_async_copy(spot, spot, v.z_r.at[mat, j, h]).wait()
            total = total + v.zr[mat, j].astype(F32)
        return total

    def small_sibling(sec):
        return pltpu.make_async_remote_copy(
            src_ref=v.sc.at[sec],
            dst_ref=v.sib,
            send_sem=v.s_s.at[0],
            recv_sem=v.s_r.at[0],
            device_id={"segment": sec},
            device_id_type=MESH,
        )

    def small_remote(sec, dl, dt):
        to_l, to_t = lax.rem(l + dl, L), lax.rem(t + dt, T)
        return pltpu.make_async_remote_copy(
            src_ref=v.sc.at[sec, to_l * T + to_t],
            dst_ref=v.scr.at[dl * T + dt],
            send_sem=v.s_s.at[dl * T + dt],
            recv_sem=v.s_r.at[dl * T + dt],
            device_id={"lat": to_t, "lon": to_l},
            device_id_type=MESH,
        )

    taps = KERNEL * KERNEL
    bias_rows = s.HID // C
    away = [(dl, dt) for dl in range(L) for dt in range(T) if dl or dt]

    def send_small(sec):
        half_rows = SMALL_ROWS // 2
        for i in range(5):
            v.sm[sec, taps + i : taps + i + 1, :] = v.vs[sec, i]
        for piece in range(s.PIECES):
            rows = jnp.concatenate(
                [
                    v.bh[sec, :, piece * s.CHUNK + j * s.CP : piece * s.CHUNK + (j + 1) * s.CP]
                    for j in range(bias_rows)
                ]
                + [jnp.zeros((SUB - bias_rows, s.CP), F32)],
                axis=0,
            )
            block = v.sm[sec, :, piece * s.CP : (piece + 1) * s.CP]
            low = jnp.concatenate(
                [block[half_rows : SMALL_ROWS - SUB], block[SMALL_ROWS - SUB :] + rows], axis=0
            )
            v.sc[sec, piece] = jnp.concatenate([block[:half_rows], low], axis=1).astype(BF16)

        @pl.when(c != sec)
        def _():
            small_sibling(sec).start()

    def merge_small(sec):
        @pl.when(c == sec)
        def _():
            pltpu.make_async_copy(v.sib, v.sib, v.s_r.at[0]).wait()
            for piece in range(s.PIECES):
                total = v.sc[sec, piece].astype(F32) + v.sib[piece].astype(F32)
                v.sc[sec, piece] = total.astype(BF16)
            for dl, dt in away:
                small_remote(sec, dl, dt).start()

    def out_remote(kind, sec, source):
        out = so_out if kind == 0 else bg_out
        return pltpu.make_async_remote_copy(
            src_ref=source,
            dst_ref=out.at[:, own_cols, :],
            send_sem=v.o_s.at[kind, 1],
            recv_sem=v.o_r.at[kind],
            device_id={"segment": sec},
            device_id_type=MESH,
        )

    def out_local(kind, source):
        out = so_out if kind == 0 else bg_out
        return pltpu.make_async_copy(source, out.at[:, own_cols, :], v.o_s.at[kind, 0])

    def send_out(kind, sec, source):
        @pl.when(c == sec)
        def _():
            out_local(kind, source).start()

        @pl.when(c != sec)
        def _():
            out_remote(kind, sec, source).start()

    def vector(sec, which):
        return v.vec[sec, which]

    def wait_param(i, sec):
        @pl.when(c == sec)
        def _():
            local_params[i].wait()

        @pl.when(c != sec)
        def _():
            src, _ = params[i]
            spot = [v.tp.at[sec]] + [v.vec.at[sec, j] for j in range(5)]
            spot = spot + [v.hbi.at[sec]]
            for h in range(HALVES):
                cols = pl.ds(h * width, width)
                spot = spot + [v.upw.at[sec, :, cols], v.dnw.at[sec, cols, :]]
            spot = spot[i]
            pltpu.make_async_remote_copy(
                src_ref=spot,
                dst_ref=spot,
                send_sem=v.prm_s.at[i],
                recv_sem=v.prm_r.at[i],
                device_id={"segment": 1 - c},
                device_id_type=MESH,
            ).wait_recv()

    STEP = 2
    CELLS = STEP * W

    def block(ref, i):
        return jnp.concatenate([ref[i * STEP + j] for j in range(STEP)], axis=0)

    def cells(i):
        return pl.ds(pl.multiple_of(i * CELLS, CELLS), CELLS)

    def transpose_into(target, source):
        for b in range(CB):
            piece = source[:, b * LANES : (b + 1) * LANES].astype(F32)
            target[b * LANES : (b + 1) * LANES, :] = piece.T.astype(BF16)

    per = s.BN // s.CHUNK

    def scatter_pieces(ref, sec, b, value):
        for j in range(per):
            index = b * per + j
            ref[sec, lax.rem(index, T), index // T] = value[:, j * s.CHUNK : (j + 1) * s.CHUNK]

    def columns(b):
        return pl.ds(pl.multiple_of(b * s.BN, s.BN), s.BN)

    def forward(sec):
        correlate(sec, sec, False)

        def norm(i, carry):
            x = jnp.concatenate([correlated(i * STEP + j) for j in range(STEP)], axis=0)
            x = x + vector(sec, 0)
            mean = jnp.sum(x, axis=-1, keepdims=True) * (1.0 / C)
            x = x - mean
            var = jnp.sum(x * x, axis=-1, keepdims=True) * (1.0 / C)
            inv = lax.rsqrt(var + EPSILON)
            unit = x * inv
            v.un[sec, cells(i), :] = unit
            v.inv[sec, cells(i), :] = jnp.broadcast_to(inv, (CELLS, LANES))
            v.nrm[cells(i), :] = (unit * vector(sec, 1) + vector(sec, 2)).astype(BF16)
            return carry

        lax.fori_loop(0, R // STEP, norm, 0)
        if sec == 1:
            transpose_into(v.nts.at[1], v.nrm)
            send_factor(2, 1)
        v.br[sec] = jnp.broadcast_to(vector(sec, 3), (M, C))

        def hidden_block(b, carry):
            before = (
                jnp.dot(v.nrm[...], v.upw[sec, :, columns(b)], preferred_element_type=F32)
                + v.hbi[sec, :, columns(b)]
            )
            active, slope = gelu_parts(before)
            v.sl[sec, b] = slope
            active = active.astype(BF16)
            scatter_pieces(v.hs, sec, b, active)
            v.br[sec] += jnp.dot(active, v.dnw[sec, columns(b), :], preferred_element_type=F32)
            return carry

        step = s.NB // HALVES
        for h in range(HALVES):
            wait_param(7 + 2 * h, sec)
            wait_param(8 + 2 * h, sec)
            lax.fori_loop(h * step, (h + 1) * step, hidden_block, 0, unroll=True)

        def finish(i, carry):
            u = block(v.nat.at[sec], i).astype(F32)
            u = (u + vector(sec, 4) * v.br[sec, cells(i), :]).astype(BF16)
            for j in range(STEP):
                row = u[j * W : (j + 1) * W]
                v.nat[sec + 1, i * STEP + j] = row
                if sec == 0:
                    write_row(1, i * STEP + j, row.astype(F32))
            return carry

        lax.fori_loop(0, R // STEP, finish, 0)

    def scale(sec, at):
        def rows(i, carry):
            g = block(v.nat.at[at], i).astype(F32)
            low = (g * vector(sec, 4)).astype(BF16)
            v.scl[sec, cells(i), :] = low
            return carry + jnp.sum(low.astype(F32), axis=0, keepdims=True)

        v.vs[sec, 3] = lax.fori_loop(0, R // STEP, rows, jnp.zeros((1, C), F32))
        transpose_into(v.sts.at[sec], v.scl.at[sec])

    def branch_sum(sec, at):
        def rows(i, carry):
            g = block(v.nat.at[at], i).astype(F32)
            return carry + jnp.sum(g * v.br[sec, cells(i), :], axis=0, keepdims=True)

        v.vs[sec, 4] = lax.fori_loop(0, R // STEP, rows, jnp.zeros((1, C), F32))

    def backward(sec, n):
        v.ng[...] = jnp.zeros((M, C), F32)

        def hidden_block(b, carry):
            grad = lax.dot_general(
                v.scl[sec], v.dnw[sec, columns(b), :], CONTRACT_LAST, preferred_element_type=F32
            )
            low = (grad * v.sl[sec, b]).astype(BF16)
            scatter_pieces(v.bs, sec, b, low)
            v.bh[sec, :, columns(b)] = jnp.sum(low.astype(F32), axis=0, keepdims=True)
            v.ng[...] += lax.dot_general(
                low, v.upw[sec, :, columns(b)], CONTRACT_LAST, preferred_element_type=F32
            )
            return carry

        lax.fori_loop(0, s.NB, hidden_block, 0, unroll=True)

        def norm(i, carry):
            bias_sum, gain_sum, shift_sum = carry
            ng = v.ng[cells(i), :]
            unit = v.un[sec, cells(i), :]
            inv = v.inv[sec, cells(i), :][:, :1]
            both = ng * unit
            gained = ng * vector(sec, 1)
            mean = jnp.sum(gained, axis=-1, keepdims=True) * (1.0 / C)
            along = jnp.sum(gained * unit, axis=-1, keepdims=True) * (1.0 / C)
            grad = (inv * (gained - mean - unit * along)).astype(BF16).astype(F32)
            for j in range(STEP):
                row = grad[j * W : (j + 1) * W]
                write_row(n, i * STEP + j, row)
                for b in range(CB):
                    lanes = row[:, b * LANES : (b + 1) * LANES]
                    v.ag[0, i * STEP + j, pl.ds(b, W, stride=CB), :] = lanes
                    v.ag[1, i * STEP + j, pl.ds(CB + b, W, stride=CB), :] = lanes
            return (
                bias_sum + jnp.sum(grad, axis=0, keepdims=True),
                gain_sum + jnp.sum(both, axis=0, keepdims=True),
                shift_sum + jnp.sum(ng, axis=0, keepdims=True),
            )

        zero = jnp.zeros((1, C), F32)
        totals = lax.fori_loop(0, R // STEP, norm, (zero, zero, zero))
        for i in range(3):
            v.vs[sec, i] = totals[i]

    def through(sec, n, at, to):
        correlate(n, sec, True)

        def rows(i, carry):
            g = v.nat[at, i].astype(F32)
            v.nat[to, i] = (g + correlated(i)).astype(BF16)
            return carry

        lax.fori_loop(0, R, rows, 0)

    load_x.wait()

    def first_rows(i, carry):
        write_row(0, i, v.nat[0, i].astype(F32))
        return carry

    lax.fori_loop(0, R, first_rows, 0)
    for sec in range(2):
        v.sm[sec] = jnp.zeros((SMALL_ROWS, C), F32)
    for i in range(R):
        v.ag[0, i, s.WC : s.ACC] = jnp.zeros((SUB, LANES), F32)
        v.ag[1, i, 0:SUB] = jnp.zeros((SUB, LANES), F32)
        v.ag[1, i, s.WC : s.ACC] = jnp.zeros((SUB, LANES), F32)
    pl.semaphore_wait(barrier, 2 * L * T - 1)
    for copy in halo_sends(0) + remote_params:
        copy.start()
    for sec in range(2):
        for i in range(7):
            wait_param(i, sec)
        for b in range(CB):
            piece = v.tp[sec, :, b * LANES : (b + 1) * LANES].astype(F32)
            v.wt[sec, pl.ds(b, taps, stride=SUB), :] = piece
            v.wt[sec, pl.ds(CB + b, taps, stride=SUB), :] = piece
    load_g.wait()
    scale(1, 3)
    send_factor(3, 1)

    forward(0)
    for copy in halo_sends(1):
        copy.start()
    send_factor(0, 0)
    transpose_into(v.nts.at[0], v.nrm)
    send_out(0, 0, v.nat.at[1])

    forward(1)
    send_factor(0, 1)
    backward(1, 2)
    for copy in halo_sends(2):
        copy.start()
    send_factor(1, 1)
    send_out(0, 1, v.nat.at[2])
    stencil(1, 1)
    branch_sum(1, 3)
    dense(1, 0)

    through(1, 2, 3, 4)
    scale(0, 4)
    send_factor(3, 0)
    send_factor(2, 0)
    backward(0, 3)
    for copy in halo_sends(3):
        copy.start()
    send_factor(1, 0)
    service(1, 0)
    dense(1, 1)
    dense(0, 0)
    send_out(1, 1, v.nat.at[4])
    branch_sum(0, 4)
    send_small(1)
    stencil(0, 0)
    send_small(0)
    merge_small(1)
    service(1, 1)
    merge_small(0)
    service(0, 0)
    dense(0, 1)
    through(0, 3, 4, 5)
    send_out(1, 0, v.nat.at[5])
    service(0, 1)

    sums = v.sc[c, l * T + t].astype(F32)
    for dl, dt in away:
        spot = v.scr.at[dl * T + dt]
        pltpu.make_async_copy(spot, spot, v.s_r.at[dl * T + dt]).wait()
        sums = sums + v.scr[dl * T + dt].astype(F32)
    total = jnp.concatenate([sums[:, : s.CP], sums[:, s.CP :]], axis=0)
    for i in range(taps):
        kg_out[i] = total[i : i + 1]
    for i in range(5):
        vg_out[i] = total[taps + i : taps + i + 1]
    for j in range(bias_rows):
        row = SMALL_ROWS - SUB + j
        hb_out[:, j * s.CP : (j + 1) * s.CP] = total[row : row + 1]
    dn_out[...] = z_total(0).T
    up_out[...] = z_total(1)

    for kind in range(2):
        any_half = v.nat.at[0]

        @pl.when(c == 0)
        def _():
            out_remote(kind, 1, any_half).wait_send()
            out_local(kind, any_half).wait()

        @pl.when(c == 1)
        def _():
            out_remote(kind, 0, any_half).wait_send()
            out_local(kind, any_half).wait()

        out = so_out if kind == 0 else bg_out
        spot = out.at[:, pl.ds(pl.multiple_of((1 - c) * W, W), W), :]
        pltpu.make_async_remote_copy(
            src_ref=spot,
            dst_ref=spot,
            send_sem=v.o_s.at[kind, 1],
            recv_sem=v.o_r.at[kind],
            device_id={"segment": 1 - c},
            device_id_type=MESH,
        ).wait_recv()
    for copy in remote_params:
        copy.wait_send()
    for n in range(4):
        for copy in halo_sends(n):
            copy.wait_send()
    for sec in range(2):
        for kind in range(4):
            factor_done(kind, sec)
    small_sibling(1 - c).wait_send()
    for dl, dt in away:
        small_remote(c, dl, dt).wait_send()
    for mat in range(2):
        for i in range(L):

            @pl.when(i != l)
            def _():
                for h in range(2):
                    z_final(mat, i, h).wait_send()


def hand_out(*refs):
    count = len(refs) // 2
    for i in range(count):
        refs[count + i][...] = refs[i][...]


def local(*args):
    inputs, up_weight = args[0], args[6]
    s = sizes(inputs.shape, up_weight.shape[2])
    scratch = scratch_of(s)
    full = pl.BlockSpec(memory_space=pltpu.VMEM)
    hbm = pl.BlockSpec(memory_space=pl.ANY)
    results = (
        pl.pallas_call(
            functools.partial(body, s, tuple(scratch)),
            out_shape=[
                jax.ShapeDtypeStruct(inputs.shape, BF16),
                jax.ShapeDtypeStruct(inputs.shape, BF16),
                jax.ShapeDtypeStruct((s.C, s.CHUNK), F32),
                jax.ShapeDtypeStruct((s.CHUNK, s.C), F32),
                jax.ShapeDtypeStruct((1, s.CHUNK), F32),
                jax.ShapeDtypeStruct((KERNEL * KERNEL, 1, s.CP), F32),
                jax.ShapeDtypeStruct((5, 1, s.CP), F32),
            ],
            in_specs=[hbm] * len(args),
            out_specs=[hbm, hbm] + [full] * 5,
            scratch_shapes=list(scratch.values()),
            compiler_params=pltpu.CompilerParams(
                collective_id=0, has_side_effects=True, vmem_limit_bytes=58 * 1024 * 1024
            ),
        )(*args)
    )
    section_out, boundary_grad, up_grad, down_grad, bias_grad, kernel_grad, vector_grad = (
        pl.pallas_call(
            hand_out,
            out_shape=[jax.ShapeDtypeStruct(x.shape, x.dtype) for x in results],
            in_specs=[full] * len(results),
            out_specs=[full] * len(results),
        )(*results)
    )
    return (
        section_out[None],
        boundary_grad[None],
        up_grad[None],
        down_grad[None],
        bias_grad,
        kernel_grad.transpose(1, 0, 2),
        vector_grad.transpose(1, 0, 2),
    )


def solution(mesh):
    placed = (
        P(("groups", "lat"), "lon", None),
        P(("groups", "lat"), "lon", None),
        P("segment", None, None),
        P("segment", None),
        P("segment", None),
        P("segment", None),
        P("segment", None, None),
        P("segment", None),
        P("segment", None, None),
        P("segment", None),
        P("segment", None),
    )
    return jax.shard_map(
        local,
        mesh=mesh,
        in_specs=placed,
        out_specs=(
            P("segment", ("groups", "lat"), "lon", None),
            P("segment", ("groups", "lat"), "lon", None),
            P(("groups", "segment"), None, ("lon", "lat")),
            P(("groups", "segment"), ("lon", "lat"), None),
            P(("groups", "segment"), ("lon", "lat")),
            P(("groups", "segment"), None, ("lon", "lat")),
            P(("groups", "segment"), None, ("lon", "lat")),
        ),
        check_vma=False,
    )
```
